256 devices in a mesh: chan: 64 (over y, z, core), hour: 4 (over x).
Axes of the slice: x: 4, y: 4, z: 8, core: 2. Of those that a mesh axis runs over, the one named last changes fastest.
Arguments:
- spectra: bfloat16 [8, 2, 8192, 2560], P('hour', None, 'chan'), may hold values from -34 to 34, as said below
- partner_lists: int32 [64, 4], replicated, may hold values from -1 to 63, as said below
- partner_counts: int32 [64], replicated, may hold values from 2 to 4, as said below
Outputs:
- stacks: float32 [256, 8, 128, 256], P(('chan', 'hour'))
The draws below stay inside these ranges and needn't reach their ends.
Inputs may be any that keep to these rules, and one draw needn't show every extreme that they name: The spectra are finite and bounded. `partner_lists`: row s lists distinct channel blocks, the first being s itself; entries from position partner_counts[s] on are -1. Within their counts, every block is listed by at most 4 rows, and some block by exactly 4. `partner_counts`: some row has exactly 4 partners.
All inputs are finite; a program needn't handle non-finite values.
Results may differ from the reference program's by a relative error of at most 0.0046.
Values may be sent and summed in bfloat16 or wider, within the bound.
A program may use at most 128 MiB of HBM per device.

```python
import math
import jax
import jax.numpy as jnp
from jax import lax

CH = 128
VS = 8
F = 2560
F0 = 64
NWIN = 8192
SMOOTH = 129
LAGS = 256
MAXP = 4
WIN = 2
BLOCKS = 64
CHANNELS = 8192
TOTWIN = 8
SLOTS = 256
N_HOUR = 4


def partner_layout(key):
    folded = jax.random.fold_in(key, 7)
    key_order, key_counts, key_start = jax.random.split(folded, 3)
    path_order = jax.random.permutation(key_order, BLOCKS).astype(jnp.int32)
    list_counts = jax.random.randint(key_counts, (BLOCKS,), MAXP // 2, MAXP + 1).astype(jnp.int32)
    run_start = jax.random.randint(key_start, (), 0, BLOCKS).astype(jnp.int32)
    path_place = (jnp.arange(BLOCKS, dtype=jnp.int32) - run_start) % BLOCKS
    path_counts = jnp.where(path_place < MAXP, jnp.maximum(list_counts, MAXP - path_place), list_counts)
    position = jnp.zeros((BLOCKS,), jnp.int32).at[path_order].set(jnp.arange(BLOCKS, dtype=jnp.int32))
    block_counts = path_counts[position]
    offsets = jnp.arange(MAXP, dtype=jnp.int32)
    partners = path_order[(position[:, None] + offsets[None, :]) % BLOCKS]
    partners = jnp.where(offsets[None, :] < block_counts[:, None], partners, -1)
    return (partners.astype(jnp.int32), block_counts.astype(jnp.int32))


def draw_partner_lists(key, part):
    return partner_layout(key)[0]


def draw_partner_counts(key, part):
    return partner_layout(key)[1]


def draw_spectra(key, part):
    full_shape = (TOTWIN, 2, CHANNELS, F)
    key_base, key_chan, key_band = jax.random.split(key, 3)
    base_noise = jnp.clip(jax.random.normal(key_base, full_shape, jnp.float32), -5.0, 5.0)
    chan_scale = jnp.exp(jax.random.uniform(key_chan, (TOTWIN, 1, CHANNELS, 1), jnp.float32, -1.2, 1.2))
    band_shape = jnp.exp(jax.random.uniform(key_band, (1, 1, 1, F), jnp.float32, -0.7, 0.7))
    drawn = base_noise * chan_scale * band_shape
    return drawn.astype(jnp.bfloat16)


def setup_inputs(seed: int = 0) -> dict:
    key_of = jax.random.split(jax.random.key(seed), 4)
    spectra = draw_spectra(jax.random.fold_in(key_of[3], 71), 0)
    partner_lists = draw_partner_lists(jax.random.fold_in(key_of[3], 71), 0)
    partner_counts = draw_partner_counts(jax.random.fold_in(key_of[3], 71), 0)
    return dict(spectra=spectra, partner_lists=partner_lists, partner_counts=partner_counts)


def whiten(real_part, imag_part):
    amplitude = jnp.sqrt(real_part * real_part + imag_part * imag_part)
    window_shape = (1,) * (amplitude.ndim - 1) + (SMOOTH,)
    padding = ((0, 0),) * (amplitude.ndim - 1) + ((SMOOTH // 2, SMOOTH // 2),)
    summed = lax.reduce_window(amplitude, jnp.zeros((), amplitude.dtype), lax.add, window_shape, (1,) * amplitude.ndim, padding)
    denominator = summed / SMOOTH + 1e-06
    return ((real_part / denominator).astype(jnp.bfloat16), (imag_part / denominator).astype(jnp.bfloat16))

def lag_table(band_bins):
    freq_index = jnp.arange(band_bins, dtype=jnp.int32)[:, None] + F0
    lag_index = jnp.arange(LAGS, dtype=jnp.int32)[None, :] - LAGS // 2
    lag_index = jnp.where(lag_index < 0, lag_index + NWIN, lag_index)
    phase_index = freq_index * lag_index % NWIN
    phase_angle = phase_index.astype(jnp.float32) * (2.0 * math.pi / NWIN)
    return jnp.concatenate([jnp.cos(phase_angle), -jnp.sin(phase_angle)], 0).astype(jnp.bfloat16)

def slot_onehot(partner_lists, partner_counts, receiver):
    offsets = jnp.arange(partner_lists.shape[1], dtype=jnp.int32)
    listed = (offsets[None, :] < partner_counts[:, None]) & (partner_lists == receiver)
    member = jnp.any(listed, axis=1)
    slot_rank = jnp.cumsum(member.astype(jnp.int32)).astype(jnp.int32) - 1
    slots = jnp.arange(partner_lists.shape[1], dtype=jnp.int32)
    return member[None, :] & (slot_rank[None, :] == slots[:, None])

def reference(spectra, partner_lists, partner_counts):
    stride = CH // VS
    source_raw = spectra[:, :, ::stride, :].astype(jnp.float32)
    src_real, src_imag = whiten(source_raw[:, 0], source_raw[:, 1])
    source_white = jnp.stack([src_real, src_imag], 1)
    table_values = lag_table(F)
    norm_scale = 1.0 / math.sqrt(4.0 * F * WIN * N_HOUR)
    block_ids = jnp.arange(BLOCKS, dtype=jnp.int32)

    def per_receiver(receiver):
        recv_block = lax.dynamic_slice_in_dim(spectra, receiver * CH, CH, 2).astype(jnp.float32)
        white_re, white_im = whiten(recv_block[:, 0], recv_block[:, 1])
        white_re = white_re.astype(jnp.float32)
        white_im = white_im.astype(jnp.float32)
        onehot = slot_onehot(partner_lists, partner_counts, receiver)
        sources_of = lax.optimization_barrier(jnp.sum(jnp.where(onehot, block_ids[None, :], 0), axis=1)).astype(jnp.int32)
        slot_used = jnp.any(onehot, axis=1)

        def per_slot(slot):
            source = lax.dynamic_slice_in_dim(source_white, sources_of[slot] * VS, VS, 2).astype(jnp.float32)
            stacked = jnp.zeros((VS, CH, LAGS), jnp.float32)
            for hour_index in range(N_HOUR):
                lower = hour_index * WIN
                sr = source[lower:lower + WIN, 0]
                si = source[lower:lower + WIN, 1]
                xr = white_re[lower:lower + WIN]
                xi = white_im[lower:lower + WIN]
                cross_re = jnp.einsum('wvf,wcf->vcf', sr, xr) + jnp.einsum('wvf,wcf->vcf', si, xi)
                cross_im = jnp.einsum('wvf,wcf->vcf', si, xr) - jnp.einsum('wvf,wcf->vcf', sr, xi)
                cross = jnp.concatenate([cross_re, cross_im], -1).astype(jnp.bfloat16).reshape(VS * CH, 2 * F)
                lagged = jnp.dot(cross, table_values, preferred_element_type=jnp.float32) * norm_scale
                stacked = stacked + lagged.reshape(VS, CH, LAGS)
            return jnp.where(slot_used[slot], stacked, jnp.zeros_like(stacked))
        return lax.map(per_slot, jnp.arange(MAXP, dtype=jnp.int32))
    result = lax.map(per_receiver, block_ids)
    return result.reshape(SLOTS, VS, CH, LAGS)
```

```python
import functools
import math

import jax
import jax.numpy as jnp
import ml_dtypes
import numpy as np
from jax import lax
from jax.experimental import pallas as pl
from jax.experimental.pallas import tpu as pltpu
from jax.sharding import PartitionSpec as P

VS = 8
CH = 128
F = 2560
F0 = 64
NWIN = 8192
SMOOTH = 129
LAGS = 256
WIN = 2
QUARTERS = 4
FQ = F // QUARTERS
GROUP = 4


def lag_table():
    bins = np.arange(F, dtype=np.int64)[:, None] + F0
    lags = np.arange(LAGS, dtype=np.int64)[None, :] - LAGS // 2
    phase = bins * (lags % NWIN) % NWIN
    angle = phase.astype(np.float32) * np.float32(2.0 * math.pi / NWIN)
    real = np.cos(angle).reshape(QUARTERS, FQ, LAGS)
    imag = -np.sin(angle).reshape(QUARTERS, FQ, LAGS)
    return np.concatenate([real, imag], 1).astype(ml_dtypes.bfloat16)


def band_matrix():
    bin_in = lax.broadcasted_iota(jnp.int32, (512, 256), 0) - 128
    bin_out = lax.broadcasted_iota(jnp.int32, (512, 256), 1)
    half = SMOOTH // 2
    inside = (bin_in - bin_out <= half) & (bin_out - bin_in <= half)
    return jnp.where(inside, 1.0, 0.0).astype(jnp.bfloat16)


def inverse_mean(real, imag, band):
    amplitude = jnp.sqrt(real * real + imag * imag)
    high = amplitude.astype(jnp.bfloat16)
    low = (amplitude - high.astype(jnp.float32)).astype(jnp.bfloat16)
    zeros = jnp.zeros((amplitude.shape[0], 128), jnp.bfloat16)
    high = jnp.concatenate([zeros, high, zeros], 1)
    low = jnp.concatenate([zeros, low, zeros], 1)
    parts = []
    for start in range(0, F, 256):
        total = jnp.dot(high[:, start:start + 512], band, preferred_element_type=jnp.float32)
        total += jnp.dot(low[:, start:start + 512], band, preferred_element_type=jnp.float32)
        parts.append(1.0 / (total / SMOOTH + 1e-06))
    return jnp.concatenate(parts, 1)


def whiten_kernel(x_ref, white_ref, source_ref):
    band = band_matrix()
    row = lax.broadcasted_iota(jnp.int32, (VS, CH), 0)
    col = lax.broadcasted_iota(jnp.int32, (VS, CH), 1)
    pick = jnp.where(col == row * (CH // VS), 1.0, 0.0).astype(jnp.bfloat16)
    for w in range(WIN):
        for c in range(0, CH, 64):
            real = x_ref[w, 0, c:c + 64, :].astype(jnp.float32)
            imag = x_ref[w, 1, c:c + 64, :].astype(jnp.float32)
            inverse = inverse_mean(real, imag, band)
            white_ref[w, 0, c:c + 64, :] = (real * inverse).astype(jnp.bfloat16)
            white_ref[w, 1, c:c + 64, :] = (imag * inverse).astype(jnp.bfloat16)
        for p in range(2):
            rows = jnp.dot(pick, white_ref[w, p], preferred_element_type=jnp.float32)
            for v in range(VS):
                source_ref[v * WIN + w, p:p + 1, :] = rows[v:v + 1].astype(jnp.bfloat16)


def whiten(x):
    return pl.pallas_call(
        whiten_kernel,
        out_shape=(
            jax.ShapeDtypeStruct((WIN, 2, CH, F), jnp.bfloat16),
            jax.ShapeDtypeStruct((VS * WIN, 2, F), jnp.bfloat16),
        ),
        in_specs=[pl.BlockSpec(memory_space=pltpu.VMEM)],
        out_specs=[pl.BlockSpec(memory_space=pltpu.VMEM)] * 2,
        compiler_params=pltpu.CompilerParams(vmem_limit_bytes=50 << 20),
    )(x)


def stack_kernel(scale, source_ref, white_ref, table_ref, out_ref, total_ref):
    def one_slot(slot, carry):
        for q in range(QUARTERS):
            bins = slice(q * FQ, (q + 1) * FQ)
            for first in range(0, VS, GROUP):
                rows = []
                for v in range(first, first + GROUP):
                    xr = [white_ref[w, 0, :, bins].reshape(8, 16, FQ) for w in range(WIN)]
                    xi = [white_ref[w, 1, :, bins].reshape(8, 16, FQ) for w in range(WIN)]
                    s = []
                    for w in range(WIN):
                        both = source_ref[(v * WIN + w) * QUARTERS + q, slot].astype(jnp.float32)
                        for p in range(2):
                            one = jnp.broadcast_to(both[p:p + 1], (16, FQ))
                            s.append(one.astype(jnp.bfloat16)[None])
                    real = (s[0] * xr[0] + s[1] * xi[0]) + (s[2] * xr[1] + s[3] * xi[1])
                    imag = (s[1] * xr[0] - s[0] * xi[0]) + (s[3] * xr[1] - s[2] * xi[1])
                    rows.append(jnp.concatenate([real.reshape(CH, FQ), imag.reshape(CH, FQ)], 1))
                lagged = jnp.dot(
                    jnp.concatenate(rows, 0), table_ref[q], preferred_element_type=jnp.float32
                )
                out = slice(first * CH, (first + GROUP) * CH)
                if q == 0:
                    total_ref[out] = lagged
                elif q < QUARTERS - 1:
                    total_ref[out] += lagged
                else:
                    out_ref[slot, out] = ((total_ref[out] + lagged) * scale).astype(jnp.bfloat16)
        return carry

    lax.fori_loop(0, out_ref.shape[0], one_slot, 0)


def stack(source, white, table, scale):
    slots = source.shape[1]
    return pl.pallas_call(
        functools.partial(stack_kernel, scale),
        out_shape=jax.ShapeDtypeStruct((slots, VS * CH, LAGS), jnp.bfloat16),
        in_specs=[pl.BlockSpec(memory_space=pltpu.VMEM)] * 3,
        out_specs=pl.BlockSpec(memory_space=pltpu.VMEM),
        scratch_shapes=[pltpu.VMEM((VS * CH, LAGS), jnp.float32)],
        compiler_params=pltpu.CompilerParams(vmem_limit_bytes=50 << 20),
    )(source, white, table)


def slot_sources(partner_lists, partner_counts):
    blocks, most = partner_lists.shape
    offsets = jnp.arange(most, dtype=jnp.int32)
    live = offsets[None, :] < partner_counts[:, None]
    receivers = jnp.arange(blocks, dtype=jnp.int32)
    member = jnp.any((partner_lists[None] == receivers[:, None, None]) & live[None], 2)
    below = receivers[:, None] < receivers[None, :]
    rank = jnp.sum(member[:, :, None] & below[None], 1, dtype=jnp.int32)
    hit = member[:, None, :] & (rank[:, None, :] == offsets[None, :, None])
    source = jnp.sum(jnp.where(hit, receivers[None, None, :], 0), 2, dtype=jnp.int32)
    return jnp.where(jnp.any(hit, 2), source, blocks)


def shards(spectra, partner_lists, partner_counts):
    blocks = partner_lists.shape[0]
    slots = partner_lists.shape[1]
    hours = lax.axis_size("hour")
    scale = 1.0 / math.sqrt(4.0 * F * WIN * hours)
    white, source = whiten(spectra)
    chunks = source.reshape(VS * WIN, 2, QUARTERS, FQ).transpose(0, 2, 1, 3)
    chunks = chunks.reshape(blocks, 2 * FQ)
    mine = lax.all_to_all(chunks, "chan", 0, 0, tiled=True)
    mine = jnp.concatenate([mine, jnp.zeros((1, 2 * FQ), jnp.bfloat16)], 0)
    wanted = slot_sources(partner_lists, partner_counts)
    chosen = mine[wanted.reshape(-1)].reshape(blocks, slots * 2 * FQ)
    arrived = lax.all_to_all(chosen, "chan", 0, 0, tiled=True)
    arrived = arrived.reshape(blocks, slots, 2, FQ)
    partial = stack(arrived, white, jnp.asarray(lag_table()), scale)
    hourly = lax.all_to_all(partial, "hour", 0, 0, tiled=True)
    total = jnp.sum(hourly.astype(jnp.float32), 0)
    return total.reshape(1, VS, CH, LAGS)


def solution(mesh):
    return jax.shard_map(
        shards,
        mesh=mesh,
        in_specs=(P("hour", None, "chan", None), P(), P()),
        out_specs=P(("chan", "hour"), None, None, None),
        check_vma=False,
    )
```

```python
import functools
import math

import jax
import jax.numpy as jnp
import ml_dtypes
import numpy as np
from jax import lax
from jax.experimental import pallas as pl
from jax.experimental.pallas import tpu as pltpu
from jax.sharding import PartitionSpec as P

VS = 8
CH = 128
F = 2560
F0 = 64
NWIN = 8192
SMOOTH = 129
LAGS = 256
WIN = 2
QUARTERS = 4
FQ = F // QUARTERS
GROUP = 4


def lag_table():
    bins = np.arange(F, dtype=np.int64)[:, None] + F0
    lags = np.arange(LAGS, dtype=np.int64)[None, :] - LAGS // 2
    phase = bins * (lags % NWIN) % NWIN
    angle = phase.astype(np.float32) * np.float32(2.0 * math.pi / NWIN)
    real = np.cos(angle).reshape(QUARTERS, FQ, LAGS)
    imag = -np.sin(angle).reshape(QUARTERS, FQ, LAGS)
    return np.concatenate([real, imag], 1).astype(ml_dtypes.bfloat16)


def band_matrix():
    bin_in = lax.broadcasted_iota(jnp.int32, (512, 256), 0) - 128
    bin_out = lax.broadcasted_iota(jnp.int32, (512, 256), 1)
    half = SMOOTH // 2
    inside = (bin_in - bin_out <= half) & (bin_out - bin_in <= half)
    return jnp.where(inside, 1.0, 0.0).astype(jnp.bfloat16)


def inverse_mean(real, imag, band):
    amplitude = jnp.sqrt(real * real + imag * imag)
    high = amplitude.astype(jnp.bfloat16)
    low = (amplitude - high.astype(jnp.float32)).astype(jnp.bfloat16)
    zeros = jnp.zeros((amplitude.shape[0], 128), jnp.bfloat16)
    high = jnp.concatenate([zeros, high, zeros], 1)
    low = jnp.concatenate([zeros, low, zeros], 1)
    parts = []
    for start in range(0, F, 256):
        total = jnp.dot(high[:, start:start + 512], band, preferred_element_type=jnp.float32)
        total += jnp.dot(low[:, start:start + 512], band, preferred_element_type=jnp.float32)
        parts.append(1.0 / (total / SMOOTH + 1e-06))
    return jnp.concatenate(parts, 1)


def pick_matrix():
    row = lax.broadcasted_iota(jnp.int32, (VS, CH), 0)
    col = lax.broadcasted_iota(jnp.int32, (VS, CH), 1)
    return jnp.where(col == row * (CH // VS), 1.0, 0.0).astype(jnp.bfloat16)


def whiten_window(x_ref, white_ref, band, w):
    for c in range(0, CH, 64):
        real = x_ref[w, 0, c:c + 64, :].astype(jnp.float32)
        imag = x_ref[w, 1, c:c + 64, :].astype(jnp.float32)
        inverse = inverse_mean(real, imag, band)
        white_ref[w, 0, c:c + 64, :] = (real * inverse).astype(jnp.bfloat16)
        white_ref[w, 1, c:c + 64, :] = (imag * inverse).astype(jnp.bfloat16)


def whiten_sources(x_ref, chunk_ref, band):
    pick = pick_matrix()
    parts = []
    for p in range(2):
        rows = [jnp.dot(pick, x_ref[w, p], preferred_element_type=jnp.float32) for w in range(WIN)]
        parts.append(jnp.concatenate(rows, 0))
    inverse = inverse_mean(parts[0], parts[1], band)
    for p in range(2):
        white = parts[p] * inverse
        for w in range(WIN):
            for v in range(VS):
                row = w * VS + v
                for q in range(QUARTERS):
                    one = white[row:row + 1, q * FQ:(q + 1) * FQ].astype(jnp.bfloat16)
                    chunk_ref[(v * WIN + w) * QUARTERS + q, p:p + 1, :] = one


def half_stack(source_ref, white_ref, table_ref, total_ref, order, first):
    for q in range(QUARTERS):
        bins = slice(q * FQ, (q + 1) * FQ)
        xr = [white_ref[w, 0, :, bins].reshape(8, 16, FQ) for w in range(WIN)]
        xi = [white_ref[w, 1, :, bins].reshape(8, 16, FQ) for w in range(WIN)]
        rows = []
        for v in range(GROUP):
            s = []
            for w in range(WIN):
                chunk = ((first + v) * WIN + w) * QUARTERS + q
                both = source_ref[order, chunk].astype(jnp.float32)
                for p in range(2):
                    one = jnp.broadcast_to(both[p:p + 1], (16, FQ))
                    s.append(one.astype(jnp.bfloat16)[None])
            real = (s[0] * xr[0] + s[1] * xi[0]) + (s[2] * xr[1] + s[3] * xi[1])
            imag = (s[1] * xr[0] - s[0] * xi[0]) + (s[3] * xr[1] - s[2] * xi[1])
            rows.append(jnp.concatenate([real.reshape(CH, FQ), imag.reshape(CH, FQ)], 1))
        lagged = jnp.dot(
            jnp.concatenate(rows, 0), table_ref[q], preferred_element_type=jnp.float32
        )
        if q == 0:
            total_ref[...] = lagged
        else:
            total_ref[...] += lagged


def fused_kernel(
    scale, blocks, hours, wanted_ref, x_ref, table_ref, out_ref,
    white_ref, chunk_ref, mine_ref, chosen_ref, source_ref, total_ref,
    far_out, far_in, near_out, near_in,
    spread_out, spread_in, slot_out, slot_in, far_out_sem, far_in_sem, near_out_sem, near_in_sem,
):
    me = lax.axis_index("chan")
    hour = lax.axis_index("hour")
    above = lax.rem(hour + 1, hours)
    below = lax.rem(hour + hours - 1, hours)
    barrier = pltpu.get_barrier_semaphore()

    def greet(k, carry):
        pl.semaphore_signal(barrier, inc=1, device_id={"chan": lax.rem(me + k, blocks)})
        return carry

    lax.fori_loop(1, blocks, greet, 0)
    for to in (above, below):
        pl.semaphore_signal(barrier, inc=1, device_id={"hour": to})

    band = band_matrix()
    whiten_sources(x_ref, chunk_ref, band)
    mine_ref[blocks] = jnp.zeros(mine_ref.shape[1:], jnp.bfloat16)
    mine_ref[me] = chunk_ref[me]
    pl.semaphore_wait(barrier, blocks + 1)

    def spread(k, carry):
        to = lax.rem(me + k, blocks)
        pltpu.make_async_remote_copy(
            chunk_ref.at[to], mine_ref.at[me], spread_out, spread_in, device_id={"chan": to}
        ).start()
        return carry

    lax.fori_loop(1, blocks, spread, 0)
    whiten_window(x_ref, white_ref, band, 0)
    others = mine_ref.at[pl.ds(0, blocks - 1)]
    pltpu.make_async_copy(others, others, spread_in).wait()

    def slot_of(order):
        return lax.rem(hour + jnp.where(order == 0, 2, jnp.where(order == 3, 0, 2 * order - 1)), hours)

    def choose(order, carry):
        slot = slot_of(order)

        def one(k, inner):
            to = lax.rem(me + k, blocks)
            chosen_ref[order, to] = mine_ref[wanted_ref[to, slot]]
            pltpu.make_async_remote_copy(
                chosen_ref.at[order, to], source_ref.at[order, me],
                slot_out.at[order], slot_in.at[order], device_id={"chan": to},
            ).start()
            return inner

        lax.fori_loop(1, blocks, one, 0)
        source_ref[order, me] = mine_ref[wanted_ref[me, slot]]
        return carry

    lax.fori_loop(0, hours, choose, 0)
    whiten_window(x_ref, white_ref, band, 1)

    def arrive(order):
        part = source_ref.at[order, pl.ds(0, blocks - 1)]
        pltpu.make_async_copy(part, part, slot_in.at[order]).wait()

    def far_copy(side, to):
        return pltpu.make_async_remote_copy(
            far_out.at[side], far_in.at[side], far_out_sem.at[side], far_in_sem.at[side],
            device_id={"hour": to},
        )

    def near_copy(side, half, to):
        return pltpu.make_async_remote_copy(
            near_out.at[side, half], near_in.at[side, half],
            near_out_sem.at[side, half], near_in_sem.at[side, half], device_id={"hour": to},
        )

    def piece(step, carry):
        order = jnp.where(step < 2, 0, jnp.where(step >= 6, 3, 1 + lax.rem(step, 2)))
        half = jnp.where((step == 2) | (step == 3), 3 - step, lax.rem(step, 2))

        for at, which in ((0, 0), (2, 1), (3, 2), (6, 3)):
            @pl.when(step == at)
            def _():
                arrive(which)

        half_stack(source_ref, white_ref, table_ref, total_ref, order, half * GROUP)

        for side, to in ((0, above), (1, below)):
            @pl.when(step == side)
            def _():
                far_out[side] = (total_ref[...] * scale).astype(jnp.bfloat16)
                far_copy(side, to).start()

            @pl.when(step == 2 + side)
            def _():
                near_out[side, 1 - side] = (total_ref[...] * scale).astype(jnp.bfloat16)
                near_copy(side, 1 - side, to).start()

            @pl.when(step == 4 + side)
            def _():
                far_copy(side, to).wait_recv()
                near_out[side, side] = (
                    total_ref[...] * scale + far_in[side].astype(jnp.float32)
                ).astype(jnp.bfloat16)
                near_copy(side, side, to).start()

            @pl.when(step == 6 + side)
            def _():
                out_ref[side] = total_ref[...] * scale

        return carry

    lax.fori_loop(0, 8, piece, 0)
    for side in (1, 0):
        near_copy(1 - side, side, above).wait_recv()
        near_copy(side, side, above).wait_recv()
        out_ref[side] += near_in[0, side].astype(jnp.float32) + near_in[1, side].astype(jnp.float32)

    others = chunk_ref.at[pl.ds(0, blocks - 1)]
    pltpu.make_async_copy(others, others, spread_out).wait()
    for order in range(hours):
        part = chosen_ref.at[order, pl.ds(0, blocks - 1)]
        pltpu.make_async_copy(part, part, slot_out.at[order]).wait()
    for side in range(2):
        far_copy(side, above).wait_send()
        for half in range(2):
            near_copy(side, half, above).wait_send()


def fused(wanted, spectra, table, scale, hours):
    blocks, slots = wanted.shape
    rows = GROUP * CH
    bf16 = jnp.bfloat16
    dma = pltpu.SemaphoreType.DMA
    return pl.pallas_call(
        functools.partial(fused_kernel, scale, blocks, hours),
        out_shape=jax.ShapeDtypeStruct((2, rows, LAGS), jnp.float32),
        in_specs=[pl.BlockSpec(memory_space=pltpu.SMEM)] + [pl.BlockSpec(memory_space=pltpu.VMEM)] * 2,
        out_specs=pl.BlockSpec(memory_space=pltpu.VMEM),
        scratch_shapes=[
            pltpu.VMEM((WIN, 2, CH, F), bf16),
            pltpu.VMEM((blocks, 2, FQ), bf16),
            pltpu.VMEM((blocks + 1, 2, FQ), bf16),
            pltpu.VMEM((slots, blocks, 2, FQ), bf16),
            pltpu.VMEM((slots, blocks, 2, FQ), bf16),
            pltpu.VMEM((rows, LAGS), jnp.float32),
            pltpu.VMEM((2, rows, LAGS), bf16),
            pltpu.VMEM((2, rows, LAGS), bf16),
            pltpu.VMEM((2, 2, rows, LAGS), bf16),
            pltpu.VMEM((2, 2, rows, LAGS), bf16),
            dma, dma, dma((slots,)), dma((slots,)), dma((2,)), dma((2,)), dma((2, 2)), dma((2, 2)),
        ],
        compiler_params=pltpu.CompilerParams(
            collective_id=0, has_side_effects=True, vmem_limit_bytes=50 << 20
        ),
    )(wanted, spectra, table)


def slot_sources(partner_lists, partner_counts):
    blocks, most = partner_lists.shape
    offsets = jnp.arange(most, dtype=jnp.int32)
    live = offsets[None, :] < partner_counts[:, None]
    receivers = jnp.arange(blocks, dtype=jnp.int32)
    member = jnp.any((partner_lists[None] == receivers[:, None, None]) & live[None], 2)
    below = receivers[:, None] < receivers[None, :]
    rank = jnp.sum(member[:, :, None] & below[None], 1, dtype=jnp.int32)
    hit = member[:, None, :] & (rank[:, None, :] == offsets[None, :, None])
    source = jnp.sum(jnp.where(hit, receivers[None, None, :], 0), 2, dtype=jnp.int32)
    return jnp.where(jnp.any(hit, 2), source, blocks)


def shards(spectra, partner_lists, partner_counts):
    hours = lax.axis_size("hour")
    scale = 1.0 / math.sqrt(4.0 * F * WIN * hours)
    wanted = slot_sources(partner_lists, partner_counts)
    stacks = fused(wanted, spectra, jnp.asarray(lag_table()), scale, hours)
    return stacks.reshape(1, VS, CH, LAGS)


def solution(mesh):
    return jax.shard_map(
        shards,
        mesh=mesh,
        in_specs=(P("hour", None, "chan", None), P(), P()),
        out_specs=P(("chan", "hour"), None, None, None),
        check_vma=False,
    )
```

```python
import functools
import math

import jax
import jax.numpy as jnp
import ml_dtypes
import numpy as np
from jax import lax
from jax.experimental import pallas as pl
from jax.experimental.pallas import tpu as pltpu
from jax.sharding import PartitionSpec as P

VS = 8
CH = 128
F = 2560
F0 = 64
NWIN = 8192
SMOOTH = 129
LAGS = 256
WIN = 2
QUARTERS = 4
FQ = F // QUARTERS
GROUP = 2


def lag_table():
    bins = np.arange(F, dtype=np.int64)[:, None] + F0
    lags = np.arange(LAGS, dtype=np.int64)[None, :] - LAGS // 2
    phase = bins * (lags % NWIN) % NWIN
    angle = phase.astype(np.float32) * np.float32(2.0 * math.pi / NWIN)
    real = np.cos(angle).reshape(QUARTERS, FQ, LAGS)
    imag = -np.sin(angle).reshape(QUARTERS, FQ, LAGS)
    return np.concatenate([real, imag], 1).astype(ml_dtypes.bfloat16)


def band_matrix():
    bin_in = lax.broadcasted_iota(jnp.int32, (512, 256), 0) - 128
    bin_out = lax.broadcasted_iota(jnp.int32, (512, 256), 1)
    half = SMOOTH // 2
    inside = (bin_in - bin_out <= half) & (bin_out - bin_in <= half)
    return jnp.where(inside, 1.0, 0.0).astype(jnp.bfloat16)


def inverse_mean(real, imag, band):
    amplitude = jnp.sqrt(real * real + imag * imag)
    high = amplitude.astype(jnp.bfloat16)
    low = (amplitude - high.astype(jnp.float32)).astype(jnp.bfloat16)
    zeros = jnp.zeros((amplitude.shape[0], 128), jnp.bfloat16)
    high = jnp.concatenate([zeros, high, zeros], 1)
    low = jnp.concatenate([zeros, low, zeros], 1)
    parts = []
    for start in range(0, F, 256):
        total = jnp.dot(high[:, start:start + 512], band, preferred_element_type=jnp.float32)
        total += jnp.dot(low[:, start:start + 512], band, preferred_element_type=jnp.float32)
        parts.append(1.0 / (total / SMOOTH + 1e-06))
    return jnp.concatenate(parts, 1)


def pick_matrix():
    row = lax.broadcasted_iota(jnp.int32, (VS, CH), 0)
    col = lax.broadcasted_iota(jnp.int32, (VS, CH), 1)
    return jnp.where(col == row * (CH // VS), 1.0, 0.0).astype(jnp.bfloat16)


def whiten_window(x_ref, white_ref, band, w):
    for c in range(0, CH, 64):
        real = x_ref[w, 0, c:c + 64, :].astype(jnp.float32)
        imag = x_ref[w, 1, c:c + 64, :].astype(jnp.float32)
        inverse = inverse_mean(real, imag, band)
        white_ref[w, 0, c:c + 64, :] = (real * inverse).astype(jnp.bfloat16)
        white_ref[w, 1, c:c + 64, :] = (imag * inverse).astype(jnp.bfloat16)


def whiten_sources(x_ref, chunk_ref, band):
    pick = pick_matrix()
    parts = []
    for p in range(2):
        rows = [jnp.dot(pick, x_ref[w, p], preferred_element_type=jnp.float32) for w in range(WIN)]
        parts.append(jnp.concatenate(rows, 0))
    inverse = inverse_mean(parts[0], parts[1], band)
    for p in range(2):
        white = parts[p] * inverse
        for w in range(WIN):
            for v in range(VS):
                row = w * VS + v
                for q in range(QUARTERS):
                    one = white[row:row + 1, q * FQ:(q + 1) * FQ].astype(jnp.bfloat16)
                    chunk_ref[(v * WIN + w) * QUARTERS + q, p:p + 1, :] = one


def piece_stack(source_ref, white_ref, table_ref, total_ref, order, first):
    for q in range(QUARTERS):
        bins = slice(q * FQ, (q + 1) * FQ)
        xr = [white_ref[w, 0, :, bins].reshape(8, 16, FQ) for w in range(WIN)]
        xi = [white_ref[w, 1, :, bins].reshape(8, 16, FQ) for w in range(WIN)]
        rows = []
        for v in range(GROUP):
            s = []
            for w in range(WIN):
                chunk = ((first + v) * WIN + w) * QUARTERS + q
                both = source_ref[order, chunk].astype(jnp.float32)
                for p in range(2):
                    one = jnp.broadcast_to(both[p:p + 1], (16, FQ))
                    s.append(one.astype(jnp.bfloat16)[None])
            real = (s[0] * xr[0] + s[1] * xi[0]) + (s[2] * xr[1] + s[3] * xi[1])
            imag = (s[1] * xr[0] - s[0] * xi[0]) + (s[3] * xr[1] - s[2] * xi[1])
            rows.append(jnp.concatenate([real.reshape(CH, FQ), imag.reshape(CH, FQ)], 1))
        lagged = jnp.dot(
            jnp.concatenate(rows, 0), table_ref[q], preferred_element_type=jnp.float32
        )
        if q == 0:
            total_ref[...] = lagged
        else:
            total_ref[...] += lagged


def fused_kernel(
    scale, blocks, hours, lists_ref, counts_ref, x_any, table_any, out_ref,
    x_ref, table_ref, white_ref, wanted_vec, wanted_ref, chunk_ref, mine_ref, chosen_ref,
    source_ref, total_ref, far_out, far_in, near_out, near_in,
    load_sem, spread_out, spread_in, slot_out, slot_in,
    far_out_sem, far_in_sem, near_out_sem, near_in_sem,
):
    me = lax.axis_index("chan")
    hour = lax.axis_index("hour")
    above = lax.rem(hour + 1, hours)
    below = lax.rem(hour + hours - 1, hours)
    barrier = pltpu.get_barrier_semaphore()

    def greet(k, carry):
        pl.semaphore_signal(barrier, inc=1, device_id={"chan": lax.rem(me + k, blocks)})
        return carry

    load_x = pltpu.make_async_copy(x_any, x_ref, load_sem.at[0])
    load_table = pltpu.make_async_copy(table_any, table_ref, load_sem.at[1])
    load_wanted = pltpu.make_async_copy(wanted_vec, wanted_ref, load_sem.at[2])
    load_x.start()
    lax.fori_loop(1, blocks, greet, 0)
    for to in (above, below):
        pl.semaphore_signal(barrier, inc=1, device_id={"hour": to})
    load_table.start()

    wanted_vec[...] = slot_table(lists_ref, counts_ref, blocks)
    load_wanted.start()
    band = band_matrix()
    load_x.wait()
    whiten_sources(x_ref, chunk_ref, band)
    mine_ref[blocks] = jnp.zeros(mine_ref.shape[1:], jnp.bfloat16)
    mine_ref[me] = chunk_ref[me]
    whiten_window(x_ref, white_ref, band, 0)
    load_wanted.wait()
    pl.semaphore_wait(barrier, blocks + 1)

    def spread(k, carry):
        to = lax.rem(me + k, blocks)
        pltpu.make_async_remote_copy(
            chunk_ref.at[to], mine_ref.at[me], spread_out, spread_in, device_id={"chan": to}
        ).start()
        return carry

    lax.fori_loop(1, blocks, spread, 0)
    whiten_window(x_ref, white_ref, band, 1)
    others = mine_ref.at[pl.ds(0, blocks - 1)]
    pltpu.make_async_copy(others, others, spread_in).wait()

    upper = me // (blocks // 2)

    def slot_of(order):
        side = lax.rem(order + upper, 2)
        away = jnp.where(order == 0, 2, jnp.where(order == 3, 0, jnp.where(side == 0, 1, 3)))
        return lax.rem(hour + away, hours)

    def choose(order, carry):
        slot = slot_of(order)

        def one(k, inner):
            to = lax.rem(me + k, blocks)
            chosen_ref[order, to] = mine_ref[wanted_ref[to, slot]]
            pltpu.make_async_remote_copy(
                chosen_ref.at[order, to], source_ref.at[order, me],
                slot_out.at[order], slot_in.at[order], device_id={"chan": to},
            ).start()
            return inner

        lax.fori_loop(1, blocks, one, 0)
        source_ref[order, me] = mine_ref[wanted_ref[me, slot]]
        return carry

    lax.fori_loop(0, hours, choose, 0)
    load_table.wait()

    def far_copy(side, sub):
        return pltpu.make_async_remote_copy(
            far_out.at[side, sub], far_in.at[side, sub],
            far_out_sem.at[side, sub], far_in_sem.at[side, sub],
            device_id={"hour": jnp.where(side == 0, above, below)},
        )

    def near_copy(side, half, sub):
        return pltpu.make_async_remote_copy(
            near_out.at[side, half, sub], near_in.at[side, half, sub],
            near_out_sem.at[side, half, sub], near_in_sem.at[side, half, sub],
            device_id={"hour": jnp.where(side == 0, above, below)},
        )

    def piece(step, carry):
        order = step // 4
        sub = lax.rem(step // 2, 2)
        side = lax.rem(step, 2)
        half = jnp.where(order == 1, 1 - side, side)

        @pl.when(lax.rem(step, 4) == 0)
        def _():
            part = source_ref.at[order, pl.ds(0, blocks - 1)]
            pltpu.make_async_copy(part, part, slot_in.at[order]).wait()

        piece_stack(source_ref, white_ref, table_ref, total_ref, order, (half * 2 + sub) * GROUP)

        @pl.when(order == 0)
        def _():
            far_out[side, sub] = (total_ref[...] * scale).astype(jnp.bfloat16)
            far_copy(side, sub).start()

        @pl.when(order == 1)
        def _():
            near_out[side, half, sub] = (total_ref[...] * scale).astype(jnp.bfloat16)
            near_copy(side, half, sub).start()

        @pl.when(order == 2)
        def _():
            far_copy(side, sub).wait_recv()
            near_out[side, half, sub] = (
                total_ref[...] * scale + far_in[side, sub].astype(jnp.float32)
            ).astype(jnp.bfloat16)
            near_copy(side, half, sub).start()

        @pl.when(order == 3)
        def _():
            out_ref[half, sub] = total_ref[...] * scale

        return carry

    lax.fori_loop(0, 16, piece, 0)
    for sub in range(2):
        for half in range(2):
            near_copy(1 - half, half, sub).wait_recv()
            near_copy(half, half, sub).wait_recv()
            out_ref[half, sub] += (
                near_in[0, half, sub].astype(jnp.float32)
                + near_in[1, half, sub].astype(jnp.float32)
            )

    others = chunk_ref.at[pl.ds(0, blocks - 1)]
    pltpu.make_async_copy(others, others, spread_out).wait()
    for order in range(hours):
        part = chosen_ref.at[order, pl.ds(0, blocks - 1)]
        pltpu.make_async_copy(part, part, slot_out.at[order]).wait()
    for side in range(2):
        for sub in range(2):
            far_copy(side, sub).wait_send()
            for half in range(2):
                near_copy(side, half, sub).wait_send()


def fused(lists, counts, spectra, table, scale, hours):
    slots, blocks = lists.shape
    lists = jnp.pad(lists, ((0, 0), (0, 128 - blocks)), constant_values=-1)
    counts = jnp.pad(counts[None], ((0, 0), (0, 128 - blocks)))
    rows = GROUP * CH
    bf16 = jnp.bfloat16
    dma = pltpu.SemaphoreType.DMA
    vmem = pl.BlockSpec(memory_space=pltpu.VMEM)
    leave = pl.BlockSpec(memory_space=pltpu.HBM)
    return pl.pallas_call(
        functools.partial(fused_kernel, scale, blocks, hours),
        out_shape=jax.ShapeDtypeStruct((2, 2, rows, LAGS), jnp.float32),
        in_specs=[vmem, vmem, leave, leave],
        out_specs=vmem,
        scratch_shapes=[
            pltpu.VMEM(spectra.shape, bf16),
            pltpu.VMEM(table.shape, bf16),
            pltpu.VMEM((WIN, 2, CH, F), bf16),
            pltpu.VMEM((blocks, 128), jnp.int32),
            pltpu.SMEM((blocks, 128), jnp.int32),
            pltpu.VMEM((blocks, 2, FQ), bf16),
            pltpu.VMEM((blocks + 1, 2, FQ), bf16),
            pltpu.VMEM((slots, blocks, 2, FQ), bf16),
            pltpu.VMEM((slots, blocks, 2, FQ), bf16),
            pltpu.VMEM((rows, LAGS), jnp.float32),
            pltpu.VMEM((2, 2, rows, LAGS), bf16),
            pltpu.VMEM((2, 2, rows, LAGS), bf16),
            pltpu.VMEM((2, 2, 2, rows, LAGS), bf16),
            pltpu.VMEM((2, 2, 2, rows, LAGS), bf16),
            dma((3,)), dma, dma, dma((slots,)), dma((slots,)),
            dma((2, 2)), dma((2, 2)), dma((2, 2, 2)), dma((2, 2, 2)),
        ],
        compiler_params=pltpu.CompilerParams(
            collective_id=0, has_side_effects=True, vmem_limit_bytes=50 << 20
        ),
    )(lists, counts, spectra, table)


def slot_table(lists_ref, counts_ref, blocks):
    most = lists_ref.shape[0]
    shape = (blocks, 128)
    receiver = lax.broadcasted_iota(jnp.int32, shape, 0)
    lane = lax.broadcasted_iota(jnp.int32, shape, 1)
    counts = jnp.broadcast_to(counts_ref[...], shape)
    member = jnp.zeros(shape, jnp.int32)
    for offset in range(most):
        listed = jnp.broadcast_to(lists_ref[offset:offset + 1, :], shape) == receiver
        member = jnp.where(listed & (offset < counts), 1, member)
    rank = member
    for step in (1, 2, 4, 8, 16, 32):
        rank = rank + jnp.where(lane >= step, pltpu.roll(rank, step, 1), 0)
    table = jnp.zeros(shape, jnp.int32)
    for slot in range(most):
        hit = (member > 0) & (rank == slot + 1)
        source = jnp.sum(jnp.where(hit, lane - blocks, 0), axis=1, keepdims=True) + blocks
        table = jnp.where(lane == slot, source, table)
    return table


def shards(spectra, partner_lists, partner_counts):
    hours = lax.axis_size("hour")
    scale = 1.0 / math.sqrt(4.0 * F * WIN * hours)
    table = jnp.asarray(lag_table())
    stacks = fused(partner_lists.T, partner_counts, spectra, table, scale, hours)
    return stacks.reshape(1, VS, CH, LAGS)


def solution(mesh):
    return jax.shard_map(
        shards,
        mesh=mesh,
        in_specs=(P("hour", None, "chan", None), P(), P()),
        out_specs=P(("chan", "hour"), None, None, None),
        check_vma=False,
    )
```

```python
import functools
import math

import jax
import jax.numpy as jnp
import ml_dtypes
import numpy as np
from jax import lax
from jax.experimental import pallas as pl
from jax.experimental.pallas import tpu as pltpu
from jax.sharding import PartitionSpec as P

VS = 8
CH = 128
F = 2560
F0 = 64
NWIN = 8192
SMOOTH = 129
LAGS = 256
WIN = 2
QUARTERS = 4
FQ = F // QUARTERS
GROUP = 2


def lag_table():
    bins = np.arange(F, dtype=np.int64)[:, None] + F0
    lags = np.arange(LAGS, dtype=np.int64)[None, :] - LAGS // 2
    phase = bins * (lags % NWIN) % NWIN
    angle = phase.astype(np.float32) * np.float32(2.0 * math.pi / NWIN)
    real = np.cos(angle).reshape(QUARTERS, FQ, LAGS)
    imag = -np.sin(angle).reshape(QUARTERS, FQ, LAGS)
    return np.concatenate([real, imag], 1).astype(ml_dtypes.bfloat16)


def band_matrix():
    bin_in = lax.broadcasted_iota(jnp.int32, (512, 256), 0) - 128
    bin_out = lax.broadcasted_iota(jnp.int32, (512, 256), 1)
    half = SMOOTH // 2
    inside = (bin_in - bin_out <= half) & (bin_out - bin_in <= half)
    return jnp.where(inside, 1.0, 0.0).astype(jnp.bfloat16)


def inverse_mean(real, imag, band):
    amplitude = jnp.sqrt(real * real + imag * imag)
    high = amplitude.astype(jnp.bfloat16)
    low = (amplitude - high.astype(jnp.float32)).astype(jnp.bfloat16)
    zeros = jnp.zeros((amplitude.shape[0], 128), jnp.bfloat16)
    high = jnp.concatenate([zeros, high, zeros], 1)
    low = jnp.concatenate([zeros, low, zeros], 1)
    parts = []
    for start in range(0, F, 256):
        total = jnp.dot(high[:, start:start + 512], band, preferred_element_type=jnp.float32)
        total += jnp.dot(low[:, start:start + 512], band, preferred_element_type=jnp.float32)
        parts.append(1.0 / (total / SMOOTH + 1e-06))
    return jnp.concatenate(parts, 1)


def pick_matrix():
    row = lax.broadcasted_iota(jnp.int32, (VS, CH), 0)
    col = lax.broadcasted_iota(jnp.int32, (VS, CH), 1)
    return jnp.where(col == row * (CH // VS), 1.0, 0.0).astype(jnp.bfloat16)


def whiten_window(x_ref, white_ref, band, w):
    for c in range(0, CH, 64):
        real = x_ref[w, 0, c:c + 64, :].astype(jnp.float32)
        imag = x_ref[w, 1, c:c + 64, :].astype(jnp.float32)
        inverse = inverse_mean(real, imag, band)
        white_ref[w, 0, c:c + 64, :] = (real * inverse).astype(jnp.bfloat16)
        white_ref[w, 1, c:c + 64, :] = (imag * inverse).astype(jnp.bfloat16)


def chunk_place(v, w, q):
    pair = v // 2
    return pair % 2, ((pair // 2 * 2 + v % 2) * WIN + w) * QUARTERS + q


def whiten_sources(x_ref, chunk_ref, band):
    pick = pick_matrix()
    parts = []
    for p in range(2):
        rows = [jnp.dot(pick, x_ref[w, p], preferred_element_type=jnp.float32) for w in range(WIN)]
        parts.append(jnp.concatenate(rows, 0))
    inverse = inverse_mean(parts[0], parts[1], band)
    for p in range(2):
        white = parts[p] * inverse
        for w in range(WIN):
            for v in range(VS):
                row = w * VS + v
                for q in range(QUARTERS):
                    one = white[row:row + 1, q * FQ:(q + 1) * FQ].astype(jnp.bfloat16)
                    core, place = chunk_place(v, w, q)
                    chunk_ref[core, place, p:p + 1, :] = one


def piece_stack(source_ref, white_ref, table_ref, total_ref, order, half, sub):
    for q in range(QUARTERS):
        bins = slice(q * FQ, (q + 1) * FQ)
        xr = [white_ref[w, 0, :, bins].reshape(8, 16, FQ) for w in range(WIN)]
        xi = [white_ref[w, 1, :, bins].reshape(8, 16, FQ) for w in range(WIN)]
        rows = []
        for v in range(GROUP):
            s = []
            for w in range(WIN):
                place = ((half * 2 + v) * WIN + w) * QUARTERS + q
                both = source_ref[order, sub, place].astype(jnp.float32)
                for p in range(2):
                    one = jnp.broadcast_to(both[p:p + 1], (16, FQ))
                    s.append(one.astype(jnp.bfloat16)[None])
            real = (s[0] * xr[0] + s[1] * xi[0]) + (s[2] * xr[1] + s[3] * xi[1])
            imag = (s[1] * xr[0] - s[0] * xi[0]) + (s[3] * xr[1] - s[2] * xi[1])
            rows.append(jnp.concatenate([real.reshape(CH, FQ), imag.reshape(CH, FQ)], 1))
        lagged = jnp.dot(
            jnp.concatenate(rows, 0), table_ref[q], preferred_element_type=jnp.float32
        )
        if q == 0:
            total_ref[...] = lagged
        else:
            total_ref[...] += lagged


def fused_kernel(
    scale, blocks, hours, lists_ref, counts_ref, x_any, table_any, out_ref,
    x_ref, table_ref, white_ref, padded_ref, wanted_vec, wanted_ref, chunk_ref, mine_ref, chosen_ref,
    source_ref, total_ref, far_out, far_in, near_out, near_in,
    load_sem, spread_out, spread_in, slot_out, slot_in,
    far_out_sem, far_in_sem, near_out_sem, near_in_sem,
):
    me = lax.axis_index("chan")
    core = lax.rem(me, 2)
    chip = me // 2
    chips = blocks // 2
    hour = lax.axis_index("hour")
    above = lax.rem(hour + 1, hours)
    below = lax.rem(hour + hours - 1, hours)
    barrier = pltpu.get_barrier_semaphore()

    def greet(k, carry):
        pl.semaphore_signal(barrier, inc=1, device_id={"chan": lax.rem(me + k, blocks)})
        return carry

    load_x = pltpu.make_async_copy(x_any, x_ref, load_sem.at[0])
    load_table = pltpu.make_async_copy(table_any, table_ref, load_sem.at[1])
    load_wanted = pltpu.make_async_copy(wanted_vec, wanted_ref, load_sem.at[2])
    load_x.start()
    lax.fori_loop(1, blocks, greet, 0)
    for to in (above, below):
        pl.semaphore_signal(barrier, inc=1, device_id={"hour": to})
    load_table.start()

    wanted_vec[...] = slot_table(lists_ref, counts_ref, padded_ref, blocks)
    load_wanted.start()
    band = band_matrix()
    load_x.wait()
    whiten_sources(x_ref, chunk_ref, band)
    mine_ref[blocks] = jnp.zeros(mine_ref.shape[1:], jnp.bfloat16)
    mine_ref[me] = chunk_ref[core, chip]
    whiten_window(x_ref, white_ref, band, 0)
    load_wanted.wait()
    pl.semaphore_wait(barrier, blocks + 1)

    for kind in range(2):
        def spread(k, carry):
            to = lax.rem(chip + k, chips)

            @pl.when((k > 0) | (core != kind))
            def _():
                pltpu.make_async_remote_copy(
                    chunk_ref.at[kind, to], mine_ref.at[me], spread_out, spread_in,
                    device_id={"chan": to * 2 + kind},
                ).start()

            return carry

        lax.fori_loop(0, chips, spread, 0)

    whiten_window(x_ref, white_ref, band, 1)
    others = mine_ref.at[pl.ds(0, blocks - 1)]
    pltpu.make_async_copy(others, others, spread_in).wait()

    upper = me // (blocks // 2)

    def slot_of(order):
        side = lax.rem(order + upper, 2)
        away = jnp.where(order == 0, 2, jnp.where(order == 3, 0, jnp.where(side == 0, 1, 3)))
        return lax.rem(hour + away, hours)

    def choose(order, carry):
        slot = slot_of(order)

        def one(k, inner):
            to = lax.rem(me + k, blocks)
            chosen_ref[order, to] = mine_ref[wanted_ref[to, slot]]
            pltpu.make_async_remote_copy(
                chosen_ref.at[order, to], source_ref.at[order, core, chip],
                slot_out.at[order], slot_in.at[order, core], device_id={"chan": to},
            ).start()
            return inner

        lax.fori_loop(1, blocks, one, 0)
        source_ref[order, core, chip] = mine_ref[wanted_ref[me, slot]]
        return carry

    lax.fori_loop(0, hours, choose, 0)
    load_table.wait()

    def far_copy(side, sub):
        return pltpu.make_async_remote_copy(
            far_out.at[side, sub], far_in.at[side, sub],
            far_out_sem.at[side, sub], far_in_sem.at[side, sub],
            device_id={"hour": jnp.where(side == 0, above, below)},
        )

    def near_copy(side, half, sub):
        return pltpu.make_async_remote_copy(
            near_out.at[side, half, sub], near_in.at[side, half, sub],
            near_out_sem.at[side, half, sub], near_in_sem.at[side, half, sub],
            device_id={"hour": jnp.where(side == 0, above, below)},
        )

    def piece(step, carry):
        order = step // 4
        sub = lax.rem(step // 2, 2)
        side = lax.rem(step, 2)
        half = jnp.where(order == 1, 1 - side, side)

        @pl.when(lax.rem(step, 2) == 0)
        def _():
            @pl.when(sub == core)
            def _():
                part = source_ref.at[order, sub, pl.ds(0, chips - 1)]
                pltpu.make_async_copy(part, part, slot_in.at[order, sub]).wait()

            @pl.when(sub != core)
            def _():
                part = source_ref.at[order, sub]
                pltpu.make_async_copy(part, part, slot_in.at[order, sub]).wait()

        piece_stack(source_ref, white_ref, table_ref, total_ref, order, half, sub)

        @pl.when(order == 0)
        def _():
            far_out[side, sub] = (total_ref[...] * scale).astype(jnp.bfloat16)
            far_copy(side, sub).start()

        @pl.when(order == 1)
        def _():
            near_out[side, half, sub] = (total_ref[...] * scale).astype(jnp.bfloat16)
            near_copy(side, half, sub).start()

        @pl.when(order == 2)
        def _():
            far_copy(side, sub).wait_recv()
            near_out[side, half, sub] = (
                total_ref[...] * scale + far_in[side, sub].astype(jnp.float32)
            ).astype(jnp.bfloat16)
            near_copy(side, half, sub).start()

        @pl.when(order == 3)
        def _():
            out_ref[half, sub] = total_ref[...] * scale

        return carry

    lax.fori_loop(0, 16, piece, 0)
    for sub in range(2):
        for half in range(2):
            near_copy(1 - half, half, sub).wait_recv()
            near_copy(half, half, sub).wait_recv()
            out_ref[half, sub] += (
                near_in[0, half, sub].astype(jnp.float32)
                + near_in[1, half, sub].astype(jnp.float32)
            )

    pltpu.make_async_copy(others, others, spread_out).wait()
    for order in range(hours):
        part = chosen_ref.at[order, pl.ds(0, blocks - 1)]
        pltpu.make_async_copy(part, part, slot_out.at[order]).wait()
    for side in range(2):
        for sub in range(2):
            far_copy(side, sub).wait_send()
            for half in range(2):
                near_copy(side, half, sub).wait_send()


def fused(lists, counts, spectra, table, scale, hours):
    slots, blocks = lists.shape
    rows = GROUP * CH
    bf16 = jnp.bfloat16
    dma = pltpu.SemaphoreType.DMA
    vmem = pl.BlockSpec(memory_space=pltpu.VMEM)
    leave = pl.BlockSpec(memory_space=pltpu.HBM)
    return pl.pallas_call(
        functools.partial(fused_kernel, scale, blocks, hours),
        out_shape=jax.ShapeDtypeStruct((2, 2, rows, LAGS), jnp.float32),
        in_specs=[vmem, vmem, leave, leave],
        out_specs=vmem,
        scratch_shapes=[
            pltpu.VMEM(spectra.shape, bf16),
            pltpu.VMEM(table.shape, bf16),
            pltpu.VMEM((WIN, 2, CH, F), bf16),
            pltpu.VMEM((8, 128), jnp.int32),
            pltpu.VMEM((blocks, 128), jnp.int32),
            pltpu.SMEM((blocks, 128), jnp.int32),
            pltpu.VMEM((2, blocks // 2, 2, FQ), bf16),
            pltpu.VMEM((blocks + 1, 2, FQ), bf16),
            pltpu.VMEM((slots, blocks, 2, FQ), bf16),
            pltpu.VMEM((slots, 2, blocks // 2, 2, FQ), bf16),
            pltpu.VMEM((rows, LAGS), jnp.float32),
            pltpu.VMEM((2, 2, rows, LAGS), bf16),
            pltpu.VMEM((2, 2, rows, LAGS), bf16),
            pltpu.VMEM((2, 2, 2, rows, LAGS), bf16),
            pltpu.VMEM((2, 2, 2, rows, LAGS), bf16),
            dma((3,)), dma, dma, dma((slots,)), dma((slots, 2)),
            dma((2, 2)), dma((2, 2)), dma((2, 2, 2)), dma((2, 2, 2)),
        ],
        compiler_params=pltpu.CompilerParams(
            collective_id=0, has_side_effects=True, vmem_limit_bytes=52 << 20
        ),
    )(lists, counts[None], spectra, table)


def slot_table(lists_ref, counts_ref, padded_ref, blocks):
    most = lists_ref.shape[0]
    shape = (blocks, 128)
    receiver = lax.broadcasted_iota(jnp.int32, shape, 0)
    lane = lax.broadcasted_iota(jnp.int32, shape, 1)
    padded_ref[...] = jnp.full(padded_ref.shape, -1, jnp.int32)
    padded_ref[:most, :blocks] = lists_ref[...]
    padded_ref[most:most + 1, :blocks] = counts_ref[...]
    counts = jnp.broadcast_to(padded_ref[most:most + 1, :], shape)
    member = jnp.zeros(shape, jnp.int32)
    for offset in range(most):
        listed = jnp.broadcast_to(padded_ref[offset:offset + 1, :], shape) == receiver
        member = jnp.where(listed & (offset < counts), 1, member)
    rank = member
    for step in (1, 2, 4, 8, 16, 32):
        rank = rank + jnp.where(lane >= step, pltpu.roll(rank, step, 1), 0)
    table = jnp.zeros(shape, jnp.int32)
    for slot in range(most):
        hit = (member > 0) & (rank == slot + 1)
        source = jnp.sum(jnp.where(hit, lane - blocks, 0), axis=1, keepdims=True) + blocks
        table = jnp.where(lane == slot, source, table)
    return table


def shards(spectra, partner_lists, partner_counts):
    hours = lax.axis_size("hour")
    scale = 1.0 / math.sqrt(4.0 * F * WIN * hours)
    table = jnp.asarray(lag_table())
    stacks = fused(partner_lists.T, partner_counts, spectra, table, scale, hours)
    return stacks.reshape(1, VS, CH, LAGS)


def solution(mesh):
    return jax.shard_map(
        shards,
        mesh=mesh,
        in_specs=(P("hour", None, "chan", None), P(), P()),
        out_specs=P(("chan", "hour"), None, None, None),
        check_vma=False,
    )
```

```python
import functools
import math

import jax
import jax.numpy as jnp
import ml_dtypes
import numpy as np
from jax import lax
from jax.experimental import pallas as pl
from jax.experimental.pallas import tpu as pltpu
from jax.sharding import PartitionSpec as P

VS = 8
CH = 128
F = 2560
F0 = 64
NWIN = 8192
SMOOTH = 129
LAGS = 256
WIN = 2
QUARTERS = 4
FQ = F // QUARTERS
GROUP = 2


def lag_table():
    bins = np.arange(F, dtype=np.int64)[:, None] + F0
    lags = np.arange(LAGS, dtype=np.int64)[None, :] - LAGS // 2
    phase = bins * (lags % NWIN) % NWIN
    angle = phase.astype(np.float32) * np.float32(2.0 * math.pi / NWIN)
    real = np.cos(angle).reshape(QUARTERS, FQ, LAGS)
    imag = -np.sin(angle).reshape(QUARTERS, FQ, LAGS)
    return np.concatenate([real, imag], 1).astype(ml_dtypes.bfloat16)


def band_matrix():
    bin_in = lax.broadcasted_iota(jnp.int32, (512, 256), 0) - 128
    bin_out = lax.broadcasted_iota(jnp.int32, (512, 256), 1)
    half = SMOOTH // 2
    inside = (bin_in - bin_out <= half) & (bin_out - bin_in <= half)
    return jnp.where(inside, 1.0, 0.0).astype(jnp.bfloat16)


def inverse_mean(real, imag, band):
    amplitude = jnp.sqrt(real * real + imag * imag)
    high = amplitude.astype(jnp.bfloat16)
    low = (amplitude - high.astype(jnp.float32)).astype(jnp.bfloat16)
    zeros = jnp.zeros((amplitude.shape[0], 128), jnp.bfloat16)
    high = jnp.concatenate([zeros, high, zeros], 1)
    low = jnp.concatenate([zeros, low, zeros], 1)
    parts = []
    for start in range(0, F, 256):
        total = jnp.dot(high[:, start:start + 512], band, preferred_element_type=jnp.float32)
        total += jnp.dot(low[:, start:start + 512], band, preferred_element_type=jnp.float32)
        parts.append(1.0 / (total / SMOOTH + 1e-06))
    return jnp.concatenate(parts, 1)


def pick_matrix():
    row = lax.broadcasted_iota(jnp.int32, (VS, CH), 0)
    col = lax.broadcasted_iota(jnp.int32, (VS, CH), 1)
    return jnp.where(col == row * (CH // VS), 1.0, 0.0).astype(jnp.bfloat16)


def whiten_window(x_ref, white_ref, band, w):
    for c in range(0, CH, 64):
        real = x_ref[w, 0, c:c + 64, :].astype(jnp.float32)
        imag = x_ref[w, 1, c:c + 64, :].astype(jnp.float32)
        inverse = inverse_mean(real, imag, band)
        white_ref[w, 0, c:c + 64, :] = (real * inverse).astype(jnp.bfloat16)
        white_ref[w, 1, c:c + 64, :] = (imag * inverse).astype(jnp.bfloat16)


def chunk_place(v, w, q):
    pair = v // 2
    return pair % 2, ((pair // 2 * 2 + v % 2) * WIN + w) * QUARTERS + q


def whiten_sources(x_ref, chunk_ref, band):
    pick = pick_matrix()
    parts = []
    for p in range(2):
        rows = [jnp.dot(pick, x_ref[w, p], preferred_element_type=jnp.float32) for w in range(WIN)]
        parts.append(jnp.concatenate(rows, 0))
    inverse = inverse_mean(parts[0], parts[1], band)
    for p in range(2):
        white = parts[p] * inverse
        for w in range(WIN):
            for v in range(VS):
                row = w * VS + v
                for q in range(QUARTERS):
                    one = white[row:row + 1, q * FQ:(q + 1) * FQ].astype(jnp.bfloat16)
                    core, place = chunk_place(v, w, q)
                    chunk_ref[core, place, p:p + 1, :] = one


def piece_stack(source_ref, white_ref, table_ref, total_ref, order, half, sub):
    for q in range(QUARTERS):
        bins = slice(q * FQ, (q + 1) * FQ)
        xr = [white_ref[w, 0, :, bins].reshape(8, 16, FQ) for w in range(WIN)]
        xi = [white_ref[w, 1, :, bins].reshape(8, 16, FQ) for w in range(WIN)]
        rows = []
        for v in range(GROUP):
            s = []
            for w in range(WIN):
                place = ((half * 2 + v) * WIN + w) * QUARTERS + q
                both = source_ref[order, sub, place].astype(jnp.float32)
                for p in range(2):
                    one = jnp.broadcast_to(both[p:p + 1], (16, FQ))
                    s.append(one.astype(jnp.bfloat16)[None])
            real = (s[0] * xr[0] + s[1] * xi[0]) + (s[2] * xr[1] + s[3] * xi[1])
            imag = (s[1] * xr[0] - s[0] * xi[0]) + (s[3] * xr[1] - s[2] * xi[1])
            rows.append(jnp.concatenate([real.reshape(CH, FQ), imag.reshape(CH, FQ)], 1))
        lagged = jnp.dot(
            jnp.concatenate(rows, 0), table_ref[q], preferred_element_type=jnp.float32
        )
        if q == 0:
            total_ref[...] = lagged
        else:
            total_ref[...] += lagged


def fused_kernel(
    scale, blocks, hours, lists_ref, counts_ref, x_any, table_any, out_ref,
    x_ref, table_ref, white_ref, padded_ref, wanted_vec, wanted_ref, chunk_ref, mine_ref, chosen_ref,
    source_ref, total_ref, far_out, far_in, near_out, near_in,
    load_sem, spread_out, spread_in, slot_out, slot_in,
    far_out_sem, far_in_sem, near_out_sem, near_in_sem,
):
    me = lax.axis_index("chan")
    core = lax.rem(me, 2)
    chip = me // 2
    chips = blocks // 2
    hour = lax.axis_index("hour")
    above = lax.rem(hour + 1, hours)
    below = lax.rem(hour + hours - 1, hours)
    barrier = pltpu.get_barrier_semaphore()

    def greet(k, carry):
        pl.semaphore_signal(barrier, inc=1, device_id={"chan": lax.rem(me + k, blocks)})
        return carry

    load_x = pltpu.make_async_copy(x_any, x_ref, load_sem.at[0])
    load_table = pltpu.make_async_copy(table_any, table_ref, load_sem.at[1])
    load_wanted = pltpu.make_async_copy(wanted_vec, wanted_ref, load_sem.at[2])
    load_x.start()
    lax.fori_loop(1, blocks, greet, 0)
    for to in (above, below):
        pl.semaphore_signal(barrier, inc=1, device_id={"hour": to})
    load_table.start()

    wanted_vec[...] = slot_table(lists_ref, counts_ref, padded_ref, blocks)
    load_wanted.start()
    band = band_matrix()
    load_x.wait()
    whiten_sources(x_ref, chunk_ref, band)
    mine_ref[blocks] = jnp.zeros(mine_ref.shape[1:], jnp.bfloat16)
    mine_ref[me] = chunk_ref[core, chip]
    whiten_window(x_ref, white_ref, band, 0)
    load_wanted.wait()
    pl.semaphore_wait(barrier, blocks + 1)

    for kind in range(2):
        def spread(k, carry):
            to = lax.rem(chip + k, chips)

            @pl.when((k > 0) | (core != kind))
            def _():
                pltpu.make_async_remote_copy(
                    chunk_ref.at[kind, to], mine_ref.at[me], spread_out, spread_in,
                    device_id={"chan": to * 2 + kind},
                ).start()

            return carry

        lax.fori_loop(0, chips, spread, 0)

    others = mine_ref.at[pl.ds(0, blocks - 1)]
    pltpu.make_async_copy(others, others, spread_in).wait()

    upper = me // (blocks // 2)

    def slot_of(order):
        side = lax.rem(order + upper, 2)
        away = jnp.where(order == 0, 2, jnp.where(order == 3, 0, jnp.where(side == 0, 1, 3)))
        return lax.rem(hour + away, hours)

    def choose(order, carry):
        slot = slot_of(order)

        def one(k, inner):
            to = lax.rem(me + k, blocks)
            chosen_ref[order, to] = mine_ref[wanted_ref[to, slot]]
            pltpu.make_async_remote_copy(
                chosen_ref.at[order, to], source_ref.at[order, core, chip],
                slot_out.at[order], slot_in.at[order, core], device_id={"chan": to},
            ).start()
            return inner

        lax.fori_loop(1, blocks, one, 0)
        source_ref[order, core, chip] = mine_ref[wanted_ref[me, slot]]
        return carry

    for stage in range(2):
        @pl.when(core == stage)
        def _():
            choose(0, 0)

        @pl.when(core != stage)
        def _():
            whiten_window(x_ref, white_ref, band, 1)

    lax.fori_loop(1, hours, choose, 0)
    load_table.wait()

    def far_copy(side, sub):
        return pltpu.make_async_remote_copy(
            far_out.at[side, sub], far_in.at[side, sub],
            far_out_sem.at[side, sub], far_in_sem.at[side, sub],
            device_id={"hour": jnp.where(side == 0, above, below)},
        )

    def near_copy(side, half, sub):
        return pltpu.make_async_remote_copy(
            near_out.at[side, half, sub], near_in.at[side, half, sub],
            near_out_sem.at[side, half, sub], near_in_sem.at[side, half, sub],
            device_id={"hour": jnp.where(side == 0, above, below)},
        )

    def piece(step, carry):
        order = step // 4
        sub = lax.rem(step // 2, 2)
        side = lax.rem(step, 2)
        half = jnp.where(order == 1, 1 - side, side)

        @pl.when(lax.rem(step, 2) == 0)
        def _():
            @pl.when(sub == core)
            def _():
                part = source_ref.at[order, sub, pl.ds(0, chips - 1)]
                pltpu.make_async_copy(part, part, slot_in.at[order, sub]).wait()

            @pl.when(sub != core)
            def _():
                part = source_ref.at[order, sub]
                pltpu.make_async_copy(part, part, slot_in.at[order, sub]).wait()

        piece_stack(source_ref, white_ref, table_ref, total_ref, order, half, sub)

        @pl.when(order == 0)
        def _():
            far_out[side, sub] = (total_ref[...] * scale).astype(jnp.bfloat16)
            far_copy(side, sub).start()

        @pl.when(order == 1)
        def _():
            near_out[side, half, sub] = (total_ref[...] * scale).astype(jnp.bfloat16)
            near_copy(side, half, sub).start()

        @pl.when(order == 2)
        def _():
            far_copy(side, sub).wait_recv()
            near_out[side, half, sub] = (
                total_ref[...] * scale + far_in[side, sub].astype(jnp.float32)
            ).astype(jnp.bfloat16)
            near_copy(side, half, sub).start()

        @pl.when(order == 3)
        def _():
            out_ref[half, sub] = total_ref[...] * scale

        return carry

    lax.fori_loop(0, 16, piece, 0)
    for sub in range(2):
        for half in range(2):
            near_copy(1 - half, half, sub).wait_recv()
            near_copy(half, half, sub).wait_recv()
            out_ref[half, sub] += (
                near_in[0, half, sub].astype(jnp.float32)
                + near_in[1, half, sub].astype(jnp.float32)
            )

    pltpu.make_async_copy(others, others, spread_out).wait()
    for order in range(hours):
        part = chosen_ref.at[order, pl.ds(0, blocks - 1)]
        pltpu.make_async_copy(part, part, slot_out.at[order]).wait()
    for side in range(2):
        for sub in range(2):
            far_copy(side, sub).wait_send()
            for half in range(2):
                near_copy(side, half, sub).wait_send()


def fused(lists, counts, spectra, table, scale, hours):
    slots, blocks = lists.shape
    rows = GROUP * CH
    bf16 = jnp.bfloat16
    dma = pltpu.SemaphoreType.DMA
    vmem = pl.BlockSpec(memory_space=pltpu.VMEM)
    leave = pl.BlockSpec(memory_space=pltpu.HBM)
    return pl.pallas_call(
        functools.partial(fused_kernel, scale, blocks, hours),
        out_shape=jax.ShapeDtypeStruct((2, 2, rows, LAGS), jnp.float32),
        in_specs=[vmem, vmem, leave, leave],
        out_specs=vmem,
        scratch_shapes=[
            pltpu.VMEM(spectra.shape, bf16),
            pltpu.VMEM(table.shape, bf16),
            pltpu.VMEM((WIN, 2, CH, F), bf16),
            pltpu.VMEM((8, 128), jnp.int32),
            pltpu.VMEM((blocks, 128), jnp.int32),
            pltpu.SMEM((blocks, 128), jnp.int32),
            pltpu.VMEM((2, blocks // 2, 2, FQ), bf16),
            pltpu.VMEM((blocks + 1, 2, FQ), bf16),
            pltpu.VMEM((slots, blocks, 2, FQ), bf16),
            pltpu.VMEM((slots, 2, blocks // 2, 2, FQ), bf16),
            pltpu.VMEM((rows, LAGS), jnp.float32),
            pltpu.VMEM((2, 2, rows, LAGS), bf16),
            pltpu.VMEM((2, 2, rows, LAGS), bf16),
            pltpu.VMEM((2, 2, 2, rows, LAGS), bf16),
            pltpu.VMEM((2, 2, 2, rows, LAGS), bf16),
            dma((3,)), dma, dma, dma((slots,)), dma((slots, 2)),
            dma((2, 2)), dma((2, 2)), dma((2, 2, 2)), dma((2, 2, 2)),
        ],
        compiler_params=pltpu.CompilerParams(
            collective_id=0, has_side_effects=True, vmem_limit_bytes=52 << 20
        ),
    )(lists, counts[None], spectra, table)


def slot_table(lists_ref, counts_ref, padded_ref, blocks):
    most = lists_ref.shape[0]
    shape = (blocks, 128)
    receiver = lax.broadcasted_iota(jnp.int32, shape, 0)
    lane = lax.broadcasted_iota(jnp.int32, shape, 1)
    padded_ref[...] = jnp.full(padded_ref.shape, -1, jnp.int32)
    padded_ref[:most, :blocks] = lists_ref[...]
    padded_ref[most:most + 1, :blocks] = counts_ref[...]
    counts = jnp.broadcast_to(padded_ref[most:most + 1, :], shape)
    member = jnp.zeros(shape, jnp.int32)
    for offset in range(most):
        listed = jnp.broadcast_to(padded_ref[offset:offset + 1, :], shape) == receiver
        member = jnp.where(listed & (offset < counts), 1, member)
    rank = member
    for step in (1, 2, 4, 8, 16, 32):
        rank = rank + jnp.where(lane >= step, pltpu.roll(rank, step, 1), 0)
    table = jnp.zeros(shape, jnp.int32)
    for slot in range(most):
        hit = (member > 0) & (rank == slot + 1)
        source = jnp.sum(jnp.where(hit, lane - blocks, 0), axis=1, keepdims=True) + blocks
        table = jnp.where(lane == slot, source, table)
    return table


def shards(spectra, partner_lists, partner_counts):
    hours = lax.axis_size("hour")
    scale = 1.0 / math.sqrt(4.0 * F * WIN * hours)
    table = jnp.asarray(lag_table())
    stacks = fused(partner_lists.T, partner_counts, spectra, table, scale, hours)
    return stacks.reshape(1, VS, CH, LAGS)


def solution(mesh):
    return jax.shard_map(
        shards,
        mesh=mesh,
        in_specs=(P("hour", None, "chan", None), P(), P()),
        out_specs=P(("chan", "hour"), None, None, None),
        check_vma=False,
    )
```

```python
import functools
import math

import jax
import jax.numpy as jnp
import ml_dtypes
import numpy as np
from jax import lax
from jax.experimental import pallas as pl
from jax.experimental.pallas import tpu as pltpu
from jax.sharding import PartitionSpec as P

VS = 8
CH = 128
F = 2560
F0 = 64
NWIN = 8192
SMOOTH = 129
LAGS = 256
WIN = 2
QUARTERS = 4
FQ = F // QUARTERS
GROUP = 2


def lag_table():
    bins = np.arange(F, dtype=np.int64)[:, None] + F0
    lags = np.arange(LAGS, dtype=np.int64)[None, :] - LAGS // 2
    phase = bins * (lags % NWIN) % NWIN
    angle = phase.astype(np.float32) * np.float32(2.0 * math.pi / NWIN)
    real = np.cos(angle).reshape(QUARTERS, FQ, LAGS)
    imag = -np.sin(angle).reshape(QUARTERS, FQ, LAGS)
    return np.concatenate([real, imag], 1).astype(ml_dtypes.bfloat16)


def band_matrix():
    bin_in = lax.broadcasted_iota(jnp.int32, (512, 256), 0) - 128
    bin_out = lax.broadcasted_iota(jnp.int32, (512, 256), 1)
    half = SMOOTH // 2
    inside = (bin_in - bin_out <= half) & (bin_out - bin_in <= half)
    return jnp.where(inside, 1.0, 0.0).astype(jnp.bfloat16)


def inverse_mean(real, imag, band):
    amplitude = jnp.sqrt(real * real + imag * imag)
    high = amplitude.astype(jnp.bfloat16)
    low = (amplitude - high.astype(jnp.float32)).astype(jnp.bfloat16)
    zeros = jnp.zeros((amplitude.shape[0], 128), jnp.bfloat16)
    high = jnp.concatenate([zeros, high, zeros], 1)
    low = jnp.concatenate([zeros, low, zeros], 1)
    parts = []
    for start in range(0, F, 256):
        total = jnp.dot(high[:, start:start + 512], band, preferred_element_type=jnp.float32)
        total += jnp.dot(low[:, start:start + 512], band, preferred_element_type=jnp.float32)
        parts.append(1.0 / (total / SMOOTH + 1e-06))
    return jnp.concatenate(parts, 1)


def pick_matrix():
    row = lax.broadcasted_iota(jnp.int32, (VS, CH), 0)
    col = lax.broadcasted_iota(jnp.int32, (VS, CH), 1)
    return jnp.where(col == row * (CH // VS), 1.0, 0.0).astype(jnp.bfloat16)


def whiten_window(x_ref, white_ref, band, w):
    for c in range(0, CH, 64):
        real = x_ref[w, 0, c:c + 64, :].astype(jnp.float32)
        imag = x_ref[w, 1, c:c + 64, :].astype(jnp.float32)
        inverse = inverse_mean(real, imag, band)
        white_ref[w, 0, c:c + 64, :] = (real * inverse).astype(jnp.bfloat16)
        white_ref[w, 1, c:c + 64, :] = (imag * inverse).astype(jnp.bfloat16)


def chunk_place(v, w, q):
    pair = v // 2
    return pair % 2, ((pair // 2 * 2 + v % 2) * WIN + w) * QUARTERS + q


def whiten_sources(x_ref, chunk_ref, band):
    pick = pick_matrix()
    parts = []
    for p in range(2):
        rows = [jnp.dot(pick, x_ref[w, p], preferred_element_type=jnp.float32) for w in range(WIN)]
        parts.append(jnp.concatenate(rows, 0))
    inverse = inverse_mean(parts[0], parts[1], band)
    for p in range(2):
        white = parts[p] * inverse
        for w in range(WIN):
            for v in range(VS):
                row = w * VS + v
                for q in range(QUARTERS):
                    one = white[row:row + 1, q * FQ:(q + 1) * FQ].astype(jnp.bfloat16)
                    core, place = chunk_place(v, w, q)
                    chunk_ref[core, place, p:p + 1, :] = one


def piece_stack(source_ref, white_ref, table_ref, total_ref, order, half, sub):
    for q in range(QUARTERS):
        bins = slice(q * FQ, (q + 1) * FQ)
        xr = [white_ref[w, 0, :, bins].reshape(8, 16, FQ) for w in range(WIN)]
        xi = [white_ref[w, 1, :, bins].reshape(8, 16, FQ) for w in range(WIN)]
        rows = []
        for v in range(GROUP):
            s = []
            for w in range(WIN):
                place = ((half * 2 + v) * WIN + w) * QUARTERS + q
                both = source_ref[order, sub, place].astype(jnp.float32)
                for p in range(2):
                    one = jnp.broadcast_to(both[p:p + 1], (16, FQ))
                    s.append(one.astype(jnp.bfloat16)[None])
            real = (s[0] * xr[0] + s[1] * xi[0]) + (s[2] * xr[1] + s[3] * xi[1])
            imag = (s[1] * xr[0] - s[0] * xi[0]) + (s[3] * xr[1] - s[2] * xi[1])
            rows.append(jnp.concatenate([real.reshape(CH, FQ), imag.reshape(CH, FQ)], 1))
        lagged = jnp.dot(
            jnp.concatenate(rows, 0), table_ref[q], preferred_element_type=jnp.float32
        )
        if q == 0:
            total_ref[...] = lagged
        else:
            total_ref[...] += lagged


def fused_kernel(
    scale, blocks, hours, lists_ref, counts_ref, x_any, table_any, out_ref,
    x_ref, table_ref, white_ref, padded_ref, wanted_vec, wanted_ref, chunk_ref, mine_ref, chosen_ref,
    source_ref, total_ref, far_out, far_in, near_out, near_in,
    load_sem, spread_out, spread_in, slot_out, slot_in,
    far_out_sem, far_in_sem, near_out_sem, near_in_sem,
):
    me = lax.axis_index("chan")
    core = lax.rem(me, 2)
    chip = me // 2
    chips = blocks // 2
    hour = lax.axis_index("hour")
    above = lax.rem(hour + 1, hours)
    below = lax.rem(hour + hours - 1, hours)
    barrier = pltpu.get_barrier_semaphore()

    def greet(k, carry):
        pl.semaphore_signal(barrier, inc=1, device_id={"chan": lax.rem(me + k, blocks)})
        return carry

    load_x = pltpu.make_async_copy(x_any, x_ref, load_sem.at[0])
    load_table = pltpu.make_async_copy(table_any, table_ref, load_sem.at[1])
    load_wanted = pltpu.make_async_copy(wanted_vec, wanted_ref, load_sem.at[2])
    load_x.start()
    lax.fori_loop(1, blocks, greet, 0)
    for to in (above, below):
        pl.semaphore_signal(barrier, inc=1, device_id={"hour": to})
    load_table.start()

    wanted_vec[...] = slot_table(lists_ref, counts_ref, padded_ref, blocks)
    load_wanted.start()
    band = band_matrix()
    load_x.wait()
    whiten_sources(x_ref, chunk_ref, band)
    mine_ref[blocks] = jnp.zeros(mine_ref.shape[1:], jnp.bfloat16)
    mine_ref[me] = chunk_ref[core, chip]
    whiten_window(x_ref, white_ref, band, 0)
    load_wanted.wait()
    pl.semaphore_wait(barrier, blocks + 1)

    for kind in range(2):
        def spread(k, carry):
            to = lax.rem(chip + k, chips)

            @pl.when((k > 0) | (core != kind))
            def _():
                pltpu.make_async_remote_copy(
                    chunk_ref.at[kind, to], mine_ref.at[me], spread_out, spread_in,
                    device_id={"chan": to * 2 + kind},
                ).start()

            return carry

        lax.fori_loop(0, chips, spread, 0)

    others = mine_ref.at[pl.ds(0, blocks - 1)]
    pltpu.make_async_copy(others, others, spread_in).wait()

    upper = me // (blocks // 2)

    def slot_of(order):
        side = lax.rem(order + upper, 2)
        away = jnp.where(order == 0, 2, jnp.where(order == 3, 0, jnp.where(side == 0, 1, 3)))
        return lax.rem(hour + away, hours)

    def choose(order, carry):
        slot = slot_of(order)

        def one(k, inner):
            to = lax.rem(me + k * 9, blocks)
            chosen_ref[order, to] = mine_ref[wanted_ref[to, slot]]
            pltpu.make_async_remote_copy(
                chosen_ref.at[order, to], source_ref.at[order, core, chip],
                slot_out.at[order], slot_in.at[order, core], device_id={"chan": to},
            ).start()
            return inner

        lax.fori_loop(1, blocks, one, 0)
        source_ref[order, core, chip] = mine_ref[wanted_ref[me, slot]]
        return carry

    for stage in range(2):
        @pl.when(core == stage)
        def _():
            choose(0, 0)

        @pl.when(core != stage)
        def _():
            whiten_window(x_ref, white_ref, band, 1)

    lax.fori_loop(1, hours, choose, 0)
    load_table.wait()

    def far_copy(side, sub):
        return pltpu.make_async_remote_copy(
            far_out.at[side, sub], far_in.at[side, sub],
            far_out_sem.at[side, sub], far_in_sem.at[side, sub],
            device_id={"hour": jnp.where(side == 0, above, below)},
        )

    def near_copy(side, half, sub):
        return pltpu.make_async_remote_copy(
            near_out.at[side, half, sub], near_in.at[side, half, sub],
            near_out_sem.at[side, half, sub], near_in_sem.at[side, half, sub],
            device_id={"hour": jnp.where(side == 0, above, below)},
        )

    def piece(step, carry):
        order = step // 4
        sub = lax.rem(step // 2, 2)
        side = lax.rem(step, 2)
        half = jnp.where(order == 1, 1 - side, side)

        @pl.when(lax.rem(step, 2) == 0)
        def _():
            @pl.when(sub == core)
            def _():
                part = source_ref.at[order, sub, pl.ds(0, chips - 1)]
                pltpu.make_async_copy(part, part, slot_in.at[order, sub]).wait()

            @pl.when(sub != core)
            def _():
                part = source_ref.at[order, sub]
                pltpu.make_async_copy(part, part, slot_in.at[order, sub]).wait()

        piece_stack(source_ref, white_ref, table_ref, total_ref, order, half, sub)

        @pl.when(order == 0)
        def _():
            far_out[side, sub] = (total_ref[...] * scale).astype(jnp.bfloat16)
            far_copy(side, sub).start()

        @pl.when(order == 1)
        def _():
            near_out[side, half, sub] = (total_ref[...] * scale).astype(jnp.bfloat16)
            near_copy(side, half, sub).start()

        @pl.when(order == 2)
        def _():
            far_copy(side, sub).wait_recv()
            near_out[side, half, sub] = (
                total_ref[...] * scale + far_in[side, sub].astype(jnp.float32)
            ).astype(jnp.bfloat16)
            near_copy(side, half, sub).start()

        @pl.when(order == 3)
        def _():
            out_ref[half, sub] = total_ref[...] * scale

        return carry

    lax.fori_loop(0, 16, piece, 0)
    for sub in range(2):
        for half in range(2):
            near_copy(1 - half, half, sub).wait_recv()
            near_copy(half, half, sub).wait_recv()
            out_ref[half, sub] += (
                near_in[0, half, sub].astype(jnp.float32)
                + near_in[1, half, sub].astype(jnp.float32)
            )

    pltpu.make_async_copy(others, others, spread_out).wait()
    for order in range(hours):
        part = chosen_ref.at[order, pl.ds(0, blocks - 1)]
        pltpu.make_async_copy(part, part, slot_out.at[order]).wait()
    for side in range(2):
        for sub in range(2):
            far_copy(side, sub).wait_send()
            for half in range(2):
                near_copy(side, half, sub).wait_send()


def fused(lists, counts, spectra, table, scale, hours):
    slots, blocks = lists.shape
    rows = GROUP * CH
    bf16 = jnp.bfloat16
    dma = pltpu.SemaphoreType.DMA
    vmem = pl.BlockSpec(memory_space=pltpu.VMEM)
    leave = pl.BlockSpec(memory_space=pltpu.HBM)
    return pl.pallas_call(
        functools.partial(fused_kernel, scale, blocks, hours),
        out_shape=jax.ShapeDtypeStruct((2, 2, rows, LAGS), jnp.float32),
        in_specs=[vmem, vmem, leave, leave],
        out_specs=vmem,
        scratch_shapes=[
            pltpu.VMEM(spectra.shape, bf16),
            pltpu.VMEM(table.shape, bf16),
            pltpu.VMEM((WIN, 2, CH, F), bf16),
            pltpu.VMEM((8, 128), jnp.int32),
            pltpu.VMEM((blocks, 128), jnp.int32),
            pltpu.SMEM((blocks, 128), jnp.int32),
            pltpu.VMEM((2, blocks // 2, 2, FQ), bf16),
            pltpu.VMEM((blocks + 1, 2, FQ), bf16),
            pltpu.VMEM((slots, blocks, 2, FQ), bf16),
            pltpu.VMEM((slots, 2, blocks // 2, 2, FQ), bf16),
            pltpu.VMEM((rows, LAGS), jnp.float32),
            pltpu.VMEM((2, 2, rows, LAGS), bf16),
            pltpu.VMEM((2, 2, rows, LAGS), bf16),
            pltpu.VMEM((2, 2, 2, rows, LAGS), bf16),
            pltpu.VMEM((2, 2, 2, rows, LAGS), bf16),
            dma((3,)), dma, dma, dma((slots,)), dma((slots, 2)),
            dma((2, 2)), dma((2, 2)), dma((2, 2, 2)), dma((2, 2, 2)),
        ],
        compiler_params=pltpu.CompilerParams(
            collective_id=0, has_side_effects=True, vmem_limit_bytes=52 << 20
        ),
    )(lists, counts[None], spectra, table)


def slot_table(lists_ref, counts_ref, padded_ref, blocks):
    most = lists_ref.shape[0]
    shape = (blocks, 128)
    receiver = lax.broadcasted_iota(jnp.int32, shape, 0)
    lane = lax.broadcasted_iota(jnp.int32, shape, 1)
    padded_ref[...] = jnp.full(padded_ref.shape, -1, jnp.int32)
    padded_ref[:most, :blocks] = lists_ref[...]
    padded_ref[most:most + 1, :blocks] = counts_ref[...]
    counts = jnp.broadcast_to(padded_ref[most:most + 1, :], shape)
    member = jnp.zeros(shape, jnp.int32)
    for offset in range(most):
        listed = jnp.broadcast_to(padded_ref[offset:offset + 1, :], shape) == receiver
        member = jnp.where(listed & (offset < counts), 1, member)
    rank = member
    for step in (1, 2, 4, 8, 16, 32):
        rank = rank + jnp.where(lane >= step, pltpu.roll(rank, step, 1), 0)
    table = jnp.zeros(shape, jnp.int32)
    for slot in range(most):
        hit = (member > 0) & (rank == slot + 1)
        source = jnp.sum(jnp.where(hit, lane - blocks, 0), axis=1, keepdims=True) + blocks
        table = jnp.where(lane == slot, source, table)
    return table


def shards(spectra, partner_lists, partner_counts):
    hours = lax.axis_size("hour")
    scale = 1.0 / math.sqrt(4.0 * F * WIN * hours)
    table = jnp.asarray(lag_table())
    stacks = fused(partner_lists.T, partner_counts, spectra, table, scale, hours)
    return stacks.reshape(1, VS, CH, LAGS)


def solution(mesh):
    return jax.shard_map(
        shards,
        mesh=mesh,
        in_specs=(P("hour", None, "chan", None), P(), P()),
        out_specs=P(("chan", "hour"), None, None, None),
        check_vma=False,
    )
```

```python
import functools
import math

import jax
import jax.numpy as jnp
import ml_dtypes
import numpy as np
from jax import lax
from jax.experimental import pallas as pl
from jax.experimental.pallas import tpu as pltpu
from jax.sharding import PartitionSpec as P

VS = 8
CH = 128
F = 2560
F0 = 64
NWIN = 8192
SMOOTH = 129
LAGS = 256
WIN = 2
QUARTERS = 4
FQ = F // QUARTERS
GROUP = 2


def lag_table():
    bins = np.arange(F, dtype=np.int64)[:, None] + F0
    lags = np.arange(LAGS, dtype=np.int64)[None, :] - LAGS // 2
    phase = bins * (lags % NWIN) % NWIN
    angle = phase.astype(np.float32) * np.float32(2.0 * math.pi / NWIN)
    real = np.cos(angle).reshape(QUARTERS, FQ, LAGS)
    imag = -np.sin(angle).reshape(QUARTERS, FQ, LAGS)
    return np.concatenate([real, imag], 1).astype(ml_dtypes.bfloat16)


def band_matrix():
    bin_in = lax.broadcasted_iota(jnp.int32, (512, 256), 0) - 128
    bin_out = lax.broadcasted_iota(jnp.int32, (512, 256), 1)
    half = SMOOTH // 2
    inside = (bin_in - bin_out <= half) & (bin_out - bin_in <= half)
    return jnp.where(inside, 1.0, 0.0).astype(jnp.bfloat16)


def inverse_mean(real, imag, band):
    amplitude = jnp.sqrt(real * real + imag * imag)
    high = amplitude.astype(jnp.bfloat16)
    low = (amplitude - high.astype(jnp.float32)).astype(jnp.bfloat16)
    zeros = jnp.zeros((amplitude.shape[0], 128), jnp.bfloat16)
    high = jnp.concatenate([zeros, high, zeros], 1)
    low = jnp.concatenate([zeros, low, zeros], 1)
    parts = []
    for start in range(0, F, 256):
        total = jnp.dot(high[:, start:start + 512], band, preferred_element_type=jnp.float32)
        total += jnp.dot(low[:, start:start + 512], band, preferred_element_type=jnp.float32)
        parts.append(1.0 / (total / SMOOTH + 1e-06))
    return jnp.concatenate(parts, 1)


def pick_matrix():
    row = lax.broadcasted_iota(jnp.int32, (VS, CH), 0)
    col = lax.broadcasted_iota(jnp.int32, (VS, CH), 1)
    return jnp.where(col == row * (CH // VS), 1.0, 0.0).astype(jnp.bfloat16)


def whiten_window(x_ref, white_ref, band, w):
    for c in range(0, CH, 64):
        real = x_ref[w, 0, c:c + 64, :].astype(jnp.float32)
        imag = x_ref[w, 1, c:c + 64, :].astype(jnp.float32)
        inverse = inverse_mean(real, imag, band)
        white_ref[w, 0, c:c + 64, :] = (real * inverse).astype(jnp.bfloat16)
        white_ref[w, 1, c:c + 64, :] = (imag * inverse).astype(jnp.bfloat16)


def chunk_place(v, w, q):
    pair = v // 2
    return pair % 2, ((pair // 2 * 2 + v % 2) * WIN + w) * QUARTERS + q


def whiten_sources(x_ref, chunk_ref, band):
    pick = pick_matrix()
    parts = []
    for p in range(2):
        rows = [jnp.dot(pick, x_ref[w, p], preferred_element_type=jnp.float32) for w in range(WIN)]
        parts.append(jnp.concatenate(rows, 0))
    inverse = inverse_mean(parts[0], parts[1], band)
    for p in range(2):
        white = parts[p] * inverse
        for w in range(WIN):
            for v in range(VS):
                row = w * VS + v
                for q in range(QUARTERS):
                    one = white[row:row + 1, q * FQ:(q + 1) * FQ].astype(jnp.bfloat16)
                    core, place = chunk_place(v, w, q)
                    chunk_ref[core, place, p:p + 1, :] = one


def piece_stack(source_ref, white_ref, table_ref, total_ref, order, half, sub):
    for q in range(QUARTERS):
        bins = slice(q * FQ, (q + 1) * FQ)
        xr = [white_ref[w, 0, :, bins].reshape(8, 16, FQ) for w in range(WIN)]
        xi = [white_ref[w, 1, :, bins].reshape(8, 16, FQ) for w in range(WIN)]
        rows = []
        for v in range(GROUP):
            s = []
            for w in range(WIN):
                place = ((half * 2 + v) * WIN + w) * QUARTERS + q
                both = source_ref[order, sub, place].astype(jnp.float32)
                for p in range(2):
                    one = jnp.broadcast_to(both[p:p + 1], (16, FQ))
                    s.append(one.astype(jnp.bfloat16)[None])
            real = (s[0] * xr[0] + s[1] * xi[0]) + (s[2] * xr[1] + s[3] * xi[1])
            imag = (s[1] * xr[0] - s[0] * xi[0]) + (s[3] * xr[1] - s[2] * xi[1])
            rows.append(jnp.concatenate([real.reshape(CH, FQ), imag.reshape(CH, FQ)], 1))
        lagged = jnp.dot(
            jnp.concatenate(rows, 0), table_ref[q], preferred_element_type=jnp.float32
        )
        if q == 0:
            total_ref[...] = lagged
        else:
            total_ref[...] += lagged


def fused_kernel(
    scale, blocks, hours, lists_ref, x_any, table_any, out_ref,
    x_ref, table_ref, white_ref, padded_ref, wanted_vec, wanted_ref, chunk_ref, mine_ref, chosen_ref,
    source_ref, total_ref, far_out, far_in, near_out, near_in,
    load_sem, spread_out, spread_in, slot_out, slot_in,
    far_out_sem, far_in_sem, near_out_sem, near_in_sem,
):
    me = lax.axis_index("chan")
    core = lax.rem(me, 2)
    chip = me // 2
    chips = blocks // 2
    hour = lax.axis_index("hour")
    above = lax.rem(hour + 1, hours)
    below = lax.rem(hour + hours - 1, hours)
    barrier = pltpu.get_barrier_semaphore()

    def greet(k, carry):
        pl.semaphore_signal(barrier, inc=1, device_id={"chan": lax.rem(me + k, blocks)})
        return carry

    load_x = pltpu.make_async_copy(x_any, x_ref, load_sem.at[0])
    load_table = pltpu.make_async_copy(table_any, table_ref, load_sem.at[1])
    load_wanted = pltpu.make_async_copy(wanted_vec, wanted_ref, load_sem.at[2])
    load_x.start()
    lax.fori_loop(1, blocks, greet, 0)
    for to in (above, below):
        pl.semaphore_signal(barrier, inc=1, device_id={"hour": to})
    load_table.start()

    wanted_vec[...] = slot_table(lists_ref, padded_ref, blocks)
    load_wanted.start()
    band = band_matrix()
    load_x.wait()
    whiten_sources(x_ref, chunk_ref, band)
    mine_ref[blocks] = jnp.zeros(mine_ref.shape[1:], jnp.bfloat16)
    mine_ref[me] = chunk_ref[core, chip]
    whiten_window(x_ref, white_ref, band, 0)
    load_wanted.wait()
    pl.semaphore_wait(barrier, blocks + 1)

    for kind in range(2):
        def spread(k, carry):
            to = lax.rem(chip + k * 9, chips)

            @pl.when((k > 0) | (core != kind))
            def _():
                pltpu.make_async_remote_copy(
                    chunk_ref.at[kind, to], mine_ref.at[me], spread_out, spread_in,
                    device_id={"chan": to * 2 + kind},
                ).start()

            return carry

        lax.fori_loop(0, chips, spread, 0)

    others = mine_ref.at[pl.ds(0, blocks - 1)]
    pltpu.make_async_copy(others, others, spread_in).wait()

    upper = me // (blocks // 2)

    def slot_of(order):
        side = lax.rem(order + upper, 2)
        away = jnp.where(order == 0, 2, jnp.where(order == 3, 0, jnp.where(side == 0, 1, 3)))
        return lax.rem(hour + away, hours)

    def choose(order, carry):
        slot = slot_of(order)

        def one(k, inner):
            to = lax.rem(me + k * 9, blocks)
            chosen_ref[order, to] = mine_ref[wanted_ref[to, slot]]
            pltpu.make_async_remote_copy(
                chosen_ref.at[order, to], source_ref.at[order, core, chip],
                slot_out.at[order], slot_in.at[order, core], device_id={"chan": to},
            ).start()
            return inner

        lax.fori_loop(1, blocks, one, 0)
        source_ref[order, core, chip] = mine_ref[wanted_ref[me, slot]]
        return carry

    for stage in range(2):
        @pl.when(core == stage)
        def _():
            choose(0, 0)

        @pl.when(core != stage)
        def _():
            whiten_window(x_ref, white_ref, band, 1)

    lax.fori_loop(1, hours, choose, 0)
    load_table.wait()

    def far_copy(side, sub):
        return pltpu.make_async_remote_copy(
            far_out.at[side, sub], far_in.at[side, sub],
            far_out_sem.at[side, sub], far_in_sem.at[side, sub],
            device_id={"hour": jnp.where(side == 0, above, below)},
        )

    def near_copy(side, half, sub):
        return pltpu.make_async_remote_copy(
            near_out.at[side, half, sub], near_in.at[side, half, sub],
            near_out_sem.at[side, half, sub], near_in_sem.at[side, half, sub],
            device_id={"hour": jnp.where(side == 0, above, below)},
        )

    def piece(step, carry):
        order = step // 4
        sub = lax.rem(step // 2, 2)
        side = lax.rem(step, 2)
        half = jnp.where(order == 1, 1 - side, side)

        @pl.when(lax.rem(step, 2) == 0)
        def _():
            @pl.when(sub == core)
            def _():
                part = source_ref.at[order, sub, pl.ds(0, chips - 1)]
                pltpu.make_async_copy(part, part, slot_in.at[order, sub]).wait()

            @pl.when(sub != core)
            def _():
                part = source_ref.at[order, sub]
                pltpu.make_async_copy(part, part, slot_in.at[order, sub]).wait()

        piece_stack(source_ref, white_ref, table_ref, total_ref, order, half, sub)

        @pl.when(order == 0)
        def _():
            far_out[side, sub] = (total_ref[...] * scale).astype(jnp.bfloat16)
            far_copy(side, sub).start()

        @pl.when(order == 1)
        def _():
            near_out[side, half, sub] = (total_ref[...] * scale).astype(jnp.bfloat16)
            near_copy(side, half, sub).start()

        @pl.when(order == 2)
        def _():
            far_copy(side, sub).wait_recv()
            near_out[side, half, sub] = (
                total_ref[...] * scale + far_in[side, sub].astype(jnp.float32)
            ).astype(jnp.bfloat16)
            near_copy(side, half, sub).start()

        @pl.when(order == 3)
        def _():
            out_ref[half, sub] = total_ref[...] * scale

        return carry

    lax.fori_loop(0, 16, piece, 0)
    for sub in range(2):
        for half in range(2):
            near_copy(1 - half, half, sub).wait_recv()
            near_copy(half, half, sub).wait_recv()
            out_ref[half, sub] += (
                near_in[0, half, sub].astype(jnp.float32)
                + near_in[1, half, sub].astype(jnp.float32)
            )

    pltpu.make_async_copy(others, others, spread_out).wait()
    for order in range(hours):
        part = chosen_ref.at[order, pl.ds(0, blocks - 1)]
        pltpu.make_async_copy(part, part, slot_out.at[order]).wait()
    for side in range(2):
        for sub in range(2):
            far_copy(side, sub).wait_send()
            for half in range(2):
                near_copy(side, half, sub).wait_send()


def fused(lists, counts, spectra, table, scale, hours):
    slots, blocks = lists.shape
    rows = GROUP * CH
    bf16 = jnp.bfloat16
    dma = pltpu.SemaphoreType.DMA
    vmem = pl.BlockSpec(memory_space=pltpu.VMEM)
    leave = pl.BlockSpec(memory_space=pltpu.HBM)
    return pl.pallas_call(
        functools.partial(fused_kernel, scale, blocks, hours),
        out_shape=jax.ShapeDtypeStruct((2, 2, rows, LAGS), jnp.float32),
        in_specs=[vmem, leave, leave],
        out_specs=vmem,
        scratch_shapes=[
            pltpu.VMEM(spectra.shape, bf16),
            pltpu.VMEM(table.shape, bf16),
            pltpu.VMEM((WIN, 2, CH, F), bf16),
            pltpu.VMEM((8, 128), jnp.int32),
            pltpu.VMEM((blocks, 128), jnp.int32),
            pltpu.SMEM((blocks, 128), jnp.int32),
            pltpu.VMEM((2, blocks // 2, 2, FQ), bf16),
            pltpu.VMEM((blocks + 1, 2, FQ), bf16),
            pltpu.VMEM((slots, blocks, 2, FQ), bf16),
            pltpu.VMEM((slots, 2, blocks // 2, 2, FQ), bf16),
            pltpu.VMEM((rows, LAGS), jnp.float32),
            pltpu.VMEM((2, 2, rows, LAGS), bf16),
            pltpu.VMEM((2, 2, rows, LAGS), bf16),
            pltpu.VMEM((2, 2, 2, rows, LAGS), bf16),
            pltpu.VMEM((2, 2, 2, rows, LAGS), bf16),
            dma((3,)), dma, dma, dma((slots,)), dma((slots, 2)),
            dma((2, 2)), dma((2, 2)), dma((2, 2, 2)), dma((2, 2, 2)),
        ],
        compiler_params=pltpu.CompilerParams(
            collective_id=0, has_side_effects=True, vmem_limit_bytes=52 << 20
        ),
    )(jnp.concatenate([lists, counts[None]], 0), spectra, table)


def slot_table(lists_ref, padded_ref, blocks):
    most = lists_ref.shape[0] - 1
    shape = (blocks, 128)
    receiver = lax.broadcasted_iota(jnp.int32, shape, 0)
    lane = lax.broadcasted_iota(jnp.int32, shape, 1)
    padded_ref[...] = jnp.full(padded_ref.shape, -1, jnp.int32)
    padded_ref[:most + 1, :blocks] = lists_ref[...]
    counts = jnp.broadcast_to(padded_ref[most:most + 1, :], shape)
    member = jnp.zeros(shape, jnp.int32)
    for offset in range(most):
        listed = jnp.broadcast_to(padded_ref[offset:offset + 1, :], shape) == receiver
        member = jnp.where(listed & (offset < counts), 1, member)
    rank = member
    for step in (1, 2, 4, 8, 16, 32):
        rank = rank + jnp.where(lane >= step, pltpu.roll(rank, step, 1), 0)
    table = jnp.zeros(shape, jnp.int32)
    for slot in range(most):
        hit = (member > 0) & (rank == slot + 1)
        source = jnp.sum(jnp.where(hit, lane - blocks, 0), axis=1, keepdims=True) + blocks
        table = jnp.where(lane == slot, source, table)
    return table


def shards(spectra, partner_lists, partner_counts):
    hours = lax.axis_size("hour")
    scale = 1.0 / math.sqrt(4.0 * F * WIN * hours)
    table = jnp.asarray(lag_table())
    stacks = fused(partner_lists.T, partner_counts, spectra, table, scale, hours)
    return stacks.reshape(1, VS, CH, LAGS)


def solution(mesh):
    return jax.shard_map(
        shards,
        mesh=mesh,
        in_specs=(P("hour", None, "chan", None), P(), P()),
        out_specs=P(("chan", "hour"), None, None, None),
        check_vma=False,
    )
```
